1024 devices in a mesh: rep: 64 (over z_lo, x, core), dom: 16 (over z_hi, y).
Axes of the slice: x: 4, y: 4, z: 32 (z_hi: 4, z_lo: 8; z = z_hi * 8 + z_lo), core: 2. Of those that a mesh axis runs over, the one named last changes fastest.
Arguments:
- block_input: bfloat16 [1024, 8, 16, 320], P(('rep', 'dom')), may hold values from -36 to 36
- cotangent: bfloat16 [1024, 8, 16, 320], P(('rep', 'dom')), may hold values from -6 to 6
- timesteps: int32 [1024], P(('rep', 'dom')), may hold values from 0 to 999
- owner_map: int32 [16], replicated, may hold values from 0 to 15, each once
- time_weight: bfloat16 [1280, 320], replicated, may hold values from -0.15625 to 0.15625
- first_weight: bfloat16 [2880, 320], P('dom'), may hold values from -0.109375 to 0.109375
- second_weight: bfloat16 [2880, 320], P('dom'), may hold values from -0.109375 to 0.109375
Outputs:
- block_output: bfloat16 [1024, 8, 16, 320], P(('rep', 'dom'))
- first_grad: float32 [2880, 320], P('dom')
- second_grad: float32 [2880, 320], P('dom')
The draws below stay inside these ranges and needn't reach their ends.
Inputs may be any that keep to these rules, and one draw needn't show every extreme that they name: `owner_map`: each dom index holds exactly one block.
All inputs are finite; a program needn't handle non-finite values.
Results may differ from the reference program's by a relative error of at most 0.0064.
Values may be sent and summed in bfloat16 or wider, within the bound.
A program may use at most 32 MiB of HBM per device.

```python
import math
import jax
import jax.numpy as jnp
from jax import lax

C = 320
GROUPS = 32
TEMB = 1280
HEIGHT = 8
WIDTH = 16
SAMPLES = 1024
DOM_BLOCKS = 16
N_DOM = 16


def draw_block_input(key, part):
    first_key, second_key, third_key = jax.random.split(key, 3)
    shape_full = (SAMPLES, HEIGHT, WIDTH, C)
    standard = jnp.clip(jax.random.normal(first_key, shape_full, jnp.float32), -6.0, 6.0)
    pixel_scale = jnp.exp(jax.random.uniform(second_key, (SAMPLES, HEIGHT, WIDTH, 1), jnp.float32, math.log(0.3), math.log(3.0)))
    channel_scale = jnp.exp(jax.random.uniform(third_key, (1, 1, 1, C), jnp.float32, math.log(0.5), math.log(2.0)))
    return (standard * pixel_scale * channel_scale).astype(jnp.bfloat16)


def touch_ends(array, rng, smallest, largest):
    extent = array.shape
    place = [jax.random.randint(jax.random.fold_in(rng, axis), (), 0, extent[axis]) for axis in range(len(extent))]
    array = array.at[tuple(place)].set(smallest)
    longest = extent.index(max(extent))
    place[longest] = (place[longest] + 1) % extent[longest]
    return array.at[tuple(place)].set(largest)


def block_scale(own_key, dims, cuts, least, largest):
    factor_of, own = 1.0, jax.random.fold_in(own_key, 6)
    for position, parts in cuts:
        heights = jnp.exp(jax.random.uniform(jax.random.fold_in(own, position), (parts,), jnp.float32, least / len(cuts), largest / len(cuts)))
        factor_of = factor_of * jnp.repeat(heights, dims[position] // parts).reshape([-1 if axis == position else 1 for axis in range(len(dims))])
    return factor_of


def normal_values(key, dims, width, bound, cuts=(), held_as=jnp.bfloat16):
    values = jax.random.normal(key, dims, jnp.float32) * width
    if len(cuts) > 0:
        values = block_scale(key, dims, cuts, -0.22, 0.18) * values
    return jnp.clip(values, min=-bound, max=bound).astype(held_as)


def setup_inputs(seed: int = 0) -> dict:
    keys = jax.random.split(jax.random.key(seed), 8)
    block_input = draw_block_input(jax.random.fold_in(keys[7], 71), 0)
    cotangent = normal_values(keys[1], (SAMPLES, HEIGHT, WIDTH, C), 1.0, 6.0, ((0, 1024),))
    timesteps = touch_ends(jax.random.randint(keys[2], (SAMPLES,), 0, 1000), jax.random.fold_in(keys[2], 1), 0, 999).astype(jnp.int32)
    owner_map = jax.random.permutation(keys[3], DOM_BLOCKS).astype(jnp.int32)
    time_weight = normal_values(keys[4], (TEMB, C), TEMB ** -0.5, 0.15625)
    first_weight = normal_values(keys[5], (9 * C, C), (9 * C) ** -0.5, 0.109375, ((0, 16),))
    second_weight = normal_values(keys[6], (9 * C, C), (9 * C) ** -0.5, 0.109375, ((0, 16),))
    return dict(block_input=block_input, cotangent=cotangent, timesteps=timesteps, owner_map=owner_map, time_weight=time_weight, first_weight=first_weight, second_weight=second_weight)


norm_eps = 1e-05

def columns(activation):
    padded = jnp.pad(activation, ((1, 1), (1, 1), (0, 0)))
    pieces = []
    for row_tap in range(3):
        for col_tap in range(3):
            pieces.append(padded[row_tap:row_tap + HEIGHT, col_tap:col_tap + WIDTH, :])
    return jnp.concatenate(pieces, axis=-1).reshape(HEIGHT * WIDTH, 9 * C)

def spread_back(gathered):
    framed = jnp.pad(gathered.reshape(HEIGHT, WIDTH, 9, C), ((1, 1), (1, 1), (0, 0), (0, 0)))
    result = jnp.zeros((HEIGHT, WIDTH, C), jnp.float32)
    for row_tap in range(3):
        for col_tap in range(3):
            result = result + framed[2 - row_tap:2 - row_tap + HEIGHT, 2 - col_tap:2 - col_tap + WIDTH, 3 * row_tap + col_tap, :]
    return result.reshape(HEIGHT * WIDTH, C)

def group_norm(values):
    grouped = values.reshape(HEIGHT * WIDTH, GROUPS, C // GROUPS)
    center = lax.optimization_barrier(jnp.mean(grouped, axis=(0, 2), keepdims=True))
    spread = lax.optimization_barrier(jnp.mean(jnp.square(grouped - center), axis=(0, 2), keepdims=True))
    inverse_std = lax.rsqrt(spread + norm_eps)
    return (((grouped - center) * inverse_std).reshape(HEIGHT * WIDTH, C), inverse_std)

def norm_back(incoming, normed, inverse_std):
    grouped_grad = incoming.reshape(HEIGHT * WIDTH, GROUPS, C // GROUPS)
    grouped_norm = normed.reshape(HEIGHT * WIDTH, GROUPS, C // GROUPS)
    mean_grad = lax.optimization_barrier(jnp.mean(grouped_grad, axis=(0, 2), keepdims=True))
    mean_prod = lax.optimization_barrier(jnp.mean(grouped_grad * grouped_norm, axis=(0, 2), keepdims=True))
    return (inverse_std * (grouped_grad - mean_grad - grouped_norm * mean_prod)).reshape(HEIGHT * WIDTH, C)

def time_bias(timestep, time_weight):
    half_dim = TEMB // 2
    frequency = jnp.exp(-math.log(10000.0) * jnp.arange(half_dim, dtype=jnp.float32) / half_dim)
    angles = timestep.astype(jnp.float32) * frequency
    embedded = jnp.concatenate([jnp.cos(angles), jnp.sin(angles)])
    activated = jax.nn.silu(embedded).astype(jnp.bfloat16)
    return jnp.dot(activated[None, :], time_weight, preferred_element_type=jnp.float32)

def logical(stored, owner_map):
    blocks = stored.reshape(N_DOM, 9 * C // N_DOM, C)
    return jnp.take(blocks, owner_map, axis=0).reshape(9 * C, C)

def to_stored(logical_grad, owner_map):
    blocks = logical_grad.reshape(N_DOM, 9 * C // N_DOM, C)
    return jnp.zeros_like(blocks).at[owner_map].set(blocks).reshape(9 * C, C)

def round_term(product):
    return lax.optimization_barrier(product.astype(jnp.bfloat16)).astype(jnp.float32)

def sample_pass(inputs_one, cotangent_one, timestep, time_weight, first_logic, second_logic):
    source = inputs_one.astype(jnp.float32).reshape(HEIGHT * WIDTH, C)
    normed, unused_std = group_norm(source)
    first_act = jax.nn.silu(normed).astype(jnp.bfloat16)
    first_cols = columns(first_act.reshape(HEIGHT, WIDTH, C))
    first_conv = jnp.dot(first_cols, first_logic, preferred_element_type=jnp.float32) + time_bias(timestep, time_weight)
    second_norm, second_std = group_norm(first_conv)
    second_act = jax.nn.silu(second_norm).astype(jnp.bfloat16)
    second_cols = columns(second_act.reshape(HEIGHT, WIDTH, C))
    output = (source + jnp.dot(second_cols, second_logic, preferred_element_type=jnp.float32)).astype(jnp.bfloat16)
    upstream = cotangent_one.reshape(HEIGHT * WIDTH, C)
    second_term = round_term(lax.dot_general(second_cols, upstream, (((0,), (0,)), ((), ())), preferred_element_type=jnp.float32))
    second_back = lax.dot_general(upstream, second_logic, (((1,), (1,)), ((), ())), preferred_element_type=jnp.float32)
    act_grad = spread_back(second_back)
    gate_value = jax.nn.sigmoid(second_norm)
    norm_grad = act_grad * gate_value * (1.0 + second_norm * (1.0 - gate_value))
    conv_grad = norm_back(norm_grad, second_norm, second_std).astype(jnp.bfloat16)
    first_term = round_term(lax.dot_general(first_cols, conv_grad, (((0,), (0,)), ((), ())), preferred_element_type=jnp.float32))
    return (output.reshape(HEIGHT, WIDTH, C), first_term, second_term)

def reference(block_input, cotangent, timesteps, owner_map, time_weight, first_weight, second_weight):
    first_logic = logical(first_weight, owner_map)
    second_logic = logical(second_weight, owner_map)

    def accumulate(totals, packed):
        inputs_one, cotangent_one, timestep = packed
        output, first_term, second_term = sample_pass(inputs_one, cotangent_one, timestep, time_weight, first_logic, second_logic)
        return ((totals[0] + first_term, totals[1] + second_term), output)
    zero_grad = jnp.zeros((9 * C, C), jnp.float32)
    totals, outputs = lax.scan(accumulate, (zero_grad, zero_grad), (block_input, cotangent, timesteps))
    first_grad = to_stored(totals[0] / SAMPLES, owner_map)
    second_grad = to_stored(totals[1] / SAMPLES, owner_map)
    return (outputs, first_grad, second_grad)
```

```python
import math

import jax
import jax.numpy as jnp
from jax import lax
from jax.experimental import pallas as pl
from jax.experimental.pallas import tpu as pltpu
from jax.sharding import PartitionSpec as P

C = 320
TEMB = 1280
HEIGHT = 8
WIDTH = 16
PIX = HEIGHT * WIDTH
NX, NY, NZH, NZL = 4, 4, 4, 8
BLOCK = 180
QROWS = 45
SAMPLES = 1024
MESH = pl.DeviceIdType.MESH
norm_eps = 1e-05
bf16 = jnp.bfloat16
f32 = jnp.float32

VM = pl.BlockSpec(memory_space=pltpu.VMEM)
SM = pl.BlockSpec(memory_space=pltpu.SMEM)


def position():
    rep, dom = lax.axis_index("rep"), lax.axis_index("dom")
    return rep // 8, lax.rem(rep // 2, 4), lax.rem(rep, 2), dom // 4, lax.rem(dom, 4)


def device(z_lo, x, core, z_hi, y):
    return {"rep": z_lo * 8 + x * 2 + core, "dom": z_hi * 4 + y}


def greet(partners):
    barrier = pltpu.get_barrier_semaphore()
    for partner in partners:
        pl.semaphore_signal(barrier, inc=1, device_id=partner, device_id_type=MESH)
    pl.semaphore_wait(barrier, len(partners))


def send(src, dst, send_sem, recv_sem, target):
    copy = pltpu.make_async_remote_copy(
        src_ref=src, dst_ref=dst, send_sem=send_sem, recv_sem=recv_sem,
        device_id=target, device_id_type=MESH,
    )
    copy.start()
    return copy


def pack_block(w):
    fold = jnp.concatenate([w[:96, 256:], jnp.pad(w[96:, 256:], ((0, 12), (0, 0)))], axis=1)
    pad = ((0, 12), (0, 0))
    return jnp.concatenate(
        [jnp.pad(w[:, :128], pad), jnp.pad(w[:, 128:256], pad), fold, jnp.zeros((32, 128), w.dtype)],
        axis=0,
    ).reshape(4, 128, 128)


def weights_kernel(own_ref, out_ref, own_sem, zs, zr, so, ro, s2, r2, s3, r3, sc, rc):
    z_lo, x, core, z_hi, y = position()
    to_z = [device(z_lo, x, core, lax.rem(z_hi + d, 4), y) for d in (1, 2, 3)]
    to_x = [device(z_lo, lax.rem(x + d, 4), core, z_hi, y) for d in (1, 2, 3)]
    to_y = [device(z_lo, x, core, z_hi, lax.rem(y + d, 4)) for d in (1, 2, 3)]
    other = device(z_lo, x, 1 - core, z_hi, y)
    keep = [pltpu.make_async_copy(own_ref.at[k], out_ref.at[k, z_hi, y], own_sem.at[k]) for k in (0, 1)]
    for copy in keep:
        copy.start()
    greet(to_z + to_x + to_y + [other])

    def run(c):
        sent = []

        def go(*copy):
            sent.append(send(*copy))
            return sent[-1]

        def arrived(copies):
            for copy in copies:
                copy.wait_recv()

        def block(d):
            return lax.rem(z_hi + 4 - d, 4)

        zc = {d: go(own_ref.at[c, x], out_ref.at[c, z_hi, y, x], zs.at[d - 1], zr.at[d - 1], to_z[d - 1]) for d in (2, 1, 3)}
        oc = [go(own_ref.at[c], out_ref.at[c, z_hi, y], so.at[j], ro.at[j], to_y[j]) for j in (1, 0, 2)]
        near, far = (to_x, to_y) if c == 0 else (to_y, to_x)

        def second(d):
            arrived([zc[d]])
            part = out_ref.at[c, block(d), y, x]
            return [go(part, part, s2.at[d - 1, j], r2.at[d - 1, j], near[j]) for j in (1, 0, 2)]

        def third(d, before):
            arrived(before)
            if c == 0:
                part = out_ref.at[0, block(d), y]
                return [go(part, part, s3.at[d - 1, 0, j], r3.at[d - 1, 0, j], far[j]) for j in (1, 0, 2)]
            copies = []
            for i in range(4):
                part = out_ref.at[1, block(d), lax.rem(y + i, 4), x]
                copies += [go(part, part, s3.at[d - 1, i, j], r3.at[d - 1, i, j], far[j]) for j in (1, 0, 2)]
            return copies

        def fourth(d, before):
            arrived(before)
            part = out_ref.at[c, block(d)]
            return [go(part, part, sc.at[d], rc.at[d], other)]

        for copy in keep:
            copy.wait()
        a1 = second(1)
        a3 = second(3)
        b1 = third(1, a1)
        b3 = third(3, a3)
        arrived(oc)
        last = []
        for i in (1, 2, 3):
            part = out_ref.at[c, z_hi, lax.rem(y + i, 4)]
            last.append(go(part, part, sc.at[3 + i], rc.at[3 + i], other))
        a2 = second(2)
        last += fourth(1, b1)
        b2 = third(2, a2)
        last += fourth(3, b3)
        last += fourth(2, b2)
        arrived(last)
        for copy in sent:
            copy.wait_send()

    for c in (0, 1):
        pl.when(core == c)(lambda c=c: run(c))


def gather_weights(own):
    dma = pltpu.SemaphoreType.DMA
    return pl.pallas_call(
        weights_kernel,
        out_shape=jax.ShapeDtypeStruct((2, NZH, NY, 4, 128, 128), bf16),
        in_specs=[VM],
        out_specs=VM,
        scratch_shapes=[
            dma((2,)), dma((3,)), dma((3,)), dma((3,)), dma((3,)), dma((3, 3)), dma((3, 3)),
            dma((3, 4, 3)), dma((3, 4, 3)), dma((7,)), dma((7,)),
        ],
        compiler_params=pltpu.CompilerParams(collective_id=0, has_side_effects=True),
        name="weights",
    )(own)


def group_matrix():
    row = lax.broadcasted_iota(jnp.int32, (C, C), 0).astype(f32)
    col = lax.broadcasted_iota(jnp.int32, (C, C), 1).astype(f32)
    same = jnp.floor((row + 0.5) * 0.1) == jnp.floor((col + 0.5) * 0.1)
    return jnp.where(same, 1.0, 0.0).astype(f32)


def shifted(v, step, rows):
    if step == 0:
        return v
    column = lax.rem(lax.broadcasted_iota(jnp.int32, (rows, C), 0), WIDTH)
    inside = (column + step >= 0) & (column + step < WIDTH)
    return jnp.where(inside, pltpu.roll(v, (-step) % rows, 0), 0.0)


def sample_kernel(
    index_ref, x_ref, cot_ref, bias_ref, w_ref, out_ref, act1_ref, grad_ref, act2_ref,
    wl1, wl2, pad,
):
    member = group_matrix()
    count = 1.0 / (PIX * 10)

    def group_mean(v):
        column = jnp.sum(v, axis=0, keepdims=True)
        return jnp.dot(
            jnp.broadcast_to(column, (8, C)), member,
            precision=lax.Precision.HIGHEST, preferred_element_type=f32,
        )[0:1] * count

    def group_norm(v):
        centered = v - group_mean(v)
        inverse_std = lax.rsqrt(group_mean(centered * centered) + norm_eps)
        return centered * inverse_std, inverse_std

    for kernel, target in ((0, wl1), (1, wl2)):
        for j in range(16):
            v = w_ref[kernel, index_ref[j]]
            base = BLOCK * j
            target[base : base + 180, 0:128] = v[0:180]
            target[base : base + 180, 128:256] = v[192:372]
            target[base : base + 96, 256:320] = v[384:480, 0:64]
            target[base + 96 : base + 180, 256:320] = v[384:468, 64:128]

    pad[:, 0:16, :] = jnp.zeros((3, 16, C), bf16)
    pad[:, 144:160, :] = jnp.zeros((3, 16, C), bf16)

    def fill(v):
        for k in range(3):
            pad[k, 16:144, :] = shifted(v, k - 1, PIX).astype(bf16)

    def conv(weight):
        total = jnp.zeros((PIX, C), f32)
        for t in range(9):
            ky, kx = t // 3, t % 3
            total = total + jnp.dot(
                pad[kx, 16 * ky : 16 * ky + PIX, :], weight[C * t : C * t + C, :],
                preferred_element_type=f32,
            )
        return total

    source = x_ref[...].astype(f32)
    normed, _ = group_norm(source)
    first_act = (normed * (1.0 / (1.0 + jnp.exp(-normed)))).astype(bf16)
    act1_ref[...] = first_act
    fill(first_act.astype(f32))
    second_norm, second_std = group_norm(conv(wl1) + bias_ref[...])
    gate = 1.0 / (1.0 + jnp.exp(-second_norm))
    second_act = (second_norm * gate).astype(bf16)
    act2_ref[...] = second_act
    fill(second_act.astype(f32))
    out_ref[...] = (source + conv(wl2)).astype(bf16)
    fill(cot_ref[...].astype(f32))
    act_grad = jnp.zeros((PIX, C), f32)
    for t in range(9):
        ky, kx = 2 - t // 3, 2 - t % 3
        act_grad = act_grad + lax.dot_general(
            pad[kx, 16 * ky : 16 * ky + PIX, :], wl2[C * t : C * t + C, :],
            (((1,), (1,)), ((), ())), preferred_element_type=f32,
        )
    norm_grad = act_grad * gate * (1.0 + second_norm * (1.0 - gate))
    grad_ref[...] = (
        second_std
        * (norm_grad - group_mean(norm_grad) - second_norm * group_mean(norm_grad * second_norm))
    ).astype(bf16)


def run_sample(index, x, cot, bias, weights):
    row = jax.ShapeDtypeStruct((PIX, C), bf16)
    return pl.pallas_call(
        sample_kernel,
        out_shape=(row, row, row, row),
        in_specs=[SM, VM, VM, VM, VM],
        out_specs=(VM, VM, VM, VM),
        scratch_shapes=[
            pltpu.VMEM((9 * C, C), bf16), pltpu.VMEM((9 * C, C), bf16), pltpu.VMEM((3, 160, C), bf16),
        ],
        name="sample",
    )(index, x, cot, bias, weights)


def exchange_kernel(act1_ref, grad_ref, act2_ref, cot_ref, acts_ref, grads_ref, own_sem, ss, rs):
    z_lo, x, core, z_hi, y = position()
    slot = x * 2 + core
    partners = [device(z_lo, x, 1 - core, z_hi, y)]
    for d in (1, 2, 3):
        for c in (0, 1):
            partners.append(device(z_lo, lax.rem(x + d, 4), c, z_hi, y))
    greet(partners)
    pairs = ((act1_ref, grad_ref), (act2_ref, cot_ref))
    outs = (acts_ref, grads_ref)
    for c in (0, 1):
        @pl.when(core == c)
        def _():
            mine = [pltpu.make_async_copy(pairs[c][a], outs[a].at[slot], own_sem.at[a]) for a in (0, 1)]
            for m in mine:
                m.start()
            copies = []
            for d in (2, 1, 3):
                for to in (0, 1):
                    for a in (0, 1):
                        copies.append(
                            send(pairs[to][a], outs[a].at[slot], ss.at[d, to, a], rs.at[d, c, a],
                                 partners[1 + (d - 1) * 2 + to])
                        )
            for a in (0, 1):
                copies.append(
                    send(pairs[1 - c][a], outs[a].at[slot], ss.at[0, 1 - c, a], rs.at[0, c, a], partners[0])
                )
            for m in mine:
                m.wait()
            for copy in copies:
                copy.wait_send()
            for d in (1, 2, 3):
                for source in (0, 1):
                    for a in (0, 1):
                        pltpu.make_async_copy(outs[a].at[slot], outs[a].at[slot], rs.at[d, source, a]).wait()
            for a in (0, 1):
                pltpu.make_async_copy(outs[a].at[slot], outs[a].at[slot], rs.at[0, 1 - c, a]).wait()


def exchange(act1, grad, act2, cot):
    dma = pltpu.SemaphoreType.DMA
    eight = jax.ShapeDtypeStruct((8, PIX, C), bf16)
    return pl.pallas_call(
        exchange_kernel,
        out_shape=(eight, eight),
        in_specs=[VM] * 4,
        out_specs=(VM, VM),
        scratch_shapes=[dma((2,)), dma((4, 2, 2)), dma((4, 2, 2))],
        compiler_params=pltpu.CompilerParams(collective_id=1, has_side_effects=True),
        name="exchange",
    )(act1, grad, act2, cot)


def gradient_kernel(start_ref, act_ref, grad_ref, out_ref, act_t, pad, total):
    for s in range(8):
        act_t[:, PIX * s : PIX * s + PIX] = act_ref[s].astype(f32).T.astype(bf16)
        pad[:, s, 0:16, :] = jnp.zeros((3, 16, C), bf16)
        pad[:, s, 144:160, :] = jnp.zeros((3, 16, C), bf16)
        v = grad_ref[s].astype(f32)
        for k in range(3):
            pad[k, s, 16:144, :] = shifted(v, k - 1, PIX).astype(bf16)
    total[9 * C :, :] = jnp.zeros((24, C), f32)

    @pl.loop(0, 9)
    def _(t):
        ky, kx = 2 - t // 3, 2 - lax.rem(t, 3)
        rows = pad[kx, :, pl.ds(pl.multiple_of(16 * ky, 16), PIX), :].reshape(8 * PIX, C)
        total[pl.ds(pl.multiple_of(C * t, 8), C), :] = jnp.dot(
            act_t[...], rows, preferred_element_type=f32
        )

    for d in range(16):
        first = start_ref[d]
        base = pl.multiple_of((first // 8) * 8, 8)
        v = pltpu.roll(total[pl.ds(base, 56), :], 56 - lax.rem(first, 8), 0)
        fold = jnp.concatenate([v[0:24, 256:320], v[24:48, 256:320]], axis=1)
        tile = jnp.concatenate([v[0:48, 0:128], v[0:48, 128:256], fold, jnp.zeros((8, 128), f32)], axis=0)
        out_ref[d % 4, d // 4] = tile.astype(bf16).reshape(NZL, 16, 128)


def run_gradient(starts, acts, grads):
    return pl.pallas_call(
        gradient_kernel,
        out_shape=jax.ShapeDtypeStruct((NY, NZH, NZL, 16, 128), bf16),
        in_specs=[SM, VM, VM],
        out_specs=VM,
        scratch_shapes=[
            pltpu.VMEM((C, 8 * PIX), bf16), pltpu.VMEM((3, 8, 160, C), bf16), pltpu.VMEM((9 * C + 24, C), f32),
        ],
        name="gradient",
    )(starts, acts, grads)


def reduce_kernel(
    part_ref, first_ref, second_ref, ybuf, s1, zbuf, s2, hbuf, final, all_ref,
    ys, yr, ls, lr, hs, hr, gs, gr, xs, xr, cs, cr, own_sem,
):
    z_lo, x, core, z_hi, y = position()
    to_y = [device(z_lo, x, core, z_hi, lax.rem(y + d, 4)) for d in (1, 2, 3)]
    to_l = [device(lax.rem(z_lo + d, 8), x, core, z_hi, y) for d in range(1, 8)]
    to_h = [device(z_lo, x, core, lax.rem(z_hi + d, 4), y) for d in (1, 2, 3)]
    to_x = [device(z_lo, lax.rem(x + d, 4), core, z_hi, y) for d in (1, 2, 3)]
    other = device(z_lo, x, 1 - core, z_hi, y)
    greet(to_y + to_l + to_h + to_x + [other])

    copies = [
        send(part_ref.at[lax.rem(y + d, 4)], ybuf.at[d - 1], ys.at[d - 1], yr.at[d - 1], to_y[d - 1])
        for d in (2, 1, 3)
    ]
    for c in copies:
        c.wait()
    for e in range(NZH):
        total = part_ref[y, e].astype(f32)
        for d in range(3):
            total = total + ybuf[d, e].astype(f32)
        s1[:, e] = total.astype(bf16)

    copies = [
        send(s1.at[lax.rem(z_lo + d, 8)], zbuf.at[d - 1], ls.at[d - 1], lr.at[d - 1], to_l[d - 1])
        for d in (4, 3, 5, 2, 6, 1, 7)
    ]
    for c in copies:
        c.wait()
    total = s1[z_lo].astype(f32)
    for d in range(7):
        total = total + zbuf[d].astype(f32)
    s2[...] = total.astype(bf16)

    copies = [
        send(s2.at[lax.rem(z_hi + d, 4)], hbuf.at[d - 1], hs.at[d - 1], hr.at[d - 1], to_h[d - 1])
        for d in (2, 1, 3)
    ]
    for c in copies:
        c.wait()
    total = s2[z_hi].astype(f32)
    for d in range(3):
        total = total + hbuf[d].astype(f32)
    final[...] = total * (1.0 / SAMPLES)

    keep = pltpu.make_async_copy(final, all_ref.at[core, x, z_lo], own_sem)
    keep.start()
    copies = [
        send(final, all_ref.at[core, x, z_lo], gs.at[d - 1], gr.at[d - 1], to_l[d - 1])
        for d in (4, 3, 5, 2, 6, 1, 7)
    ]
    keep.wait()
    for c in copies:
        c.wait()
    quarter = all_ref.at[core, x]
    copies = [send(quarter, quarter, xs.at[d - 1], xr.at[d - 1], to_x[d - 1]) for d in (2, 1, 3)]
    for c in copies:
        c.wait()
    whole = all_ref.at[core]
    send(whole, whole, cs, cr, other).wait()

    for kernel, target in ((0, first_ref), (1, second_ref)):
        for q in range(4):
            v = all_ref[kernel, q].reshape(128, 128)
            base = QROWS * q
            target[base : base + 45, 0:128] = v[0:45]
            target[base : base + 45, 128:256] = v[48:93]
            target[base : base + 24, 256:320] = v[96:120, 0:64]
            target[base + 24 : base + 45, 256:320] = v[96:117, 64:128]


def reduce_all(part):
    dma = pltpu.SemaphoreType.DMA
    out = jax.ShapeDtypeStruct((BLOCK, C), f32)
    return pl.pallas_call(
        reduce_kernel,
        out_shape=(out, out),
        in_specs=[VM],
        out_specs=(VM, VM),
        scratch_shapes=[
            pltpu.VMEM((3, NZH, NZL, 16, 128), bf16),
            pltpu.VMEM((NZL, NZH, 16, 128), bf16),
            pltpu.VMEM((7, NZH, 16, 128), bf16),
            pltpu.VMEM((NZH, 16, 128), bf16),
            pltpu.VMEM((3, 16, 128), bf16),
            pltpu.VMEM((16, 128), f32),
            pltpu.VMEM((2, NX, NZL, 16, 128), f32),
            dma((3,)), dma((3,)), dma((7,)), dma((7,)), dma((3,)), dma((3,)),
            dma((7,)), dma((7,)), dma((3,)), dma((3,)), dma, dma, dma,
        ],
        compiler_params=pltpu.CompilerParams(collective_id=2, has_side_effects=True),
        name="reduce",
    )(part)


def time_bias(timestep, time_weight):
    half_dim = TEMB // 2
    frequency = jnp.exp(-math.log(10000.0) * jnp.arange(half_dim, dtype=f32) / half_dim)
    angles = timestep.astype(f32) * frequency
    embedded = jnp.concatenate([jnp.cos(angles), jnp.sin(angles)])
    activated = jax.nn.silu(embedded).astype(bf16)
    return jnp.dot(activated[None, :], time_weight, preferred_element_type=f32)


def body(block_input, cotangent, timesteps, owner_map, time_weight, first_weight, second_weight):
    own = jnp.stack([pack_block(first_weight), pack_block(second_weight)])
    ids = jnp.arange(16, dtype=jnp.int32)
    inverse = jnp.sum((owner_map[None, :] == ids[:, None]).astype(jnp.int32) * ids[None, :], axis=1)
    quarter = lax.rem(lax.axis_index("rep") // 2, 4)
    starts = inverse * BLOCK + quarter.astype(jnp.int32) * QROWS
    bias = time_bias(timesteps[0], time_weight)
    weights = gather_weights(own).reshape(2, 16, 512, 128)
    x = block_input.reshape(PIX, C)
    cot = cotangent.reshape(PIX, C)
    out, act1, grad, act2 = run_sample(owner_map, x, cot, bias, weights)
    acts, grads = exchange(act1, grad, act2, cot)
    part = run_gradient(starts, acts, grads)
    first_grad, second_grad = reduce_all(part)
    return out.reshape(1, HEIGHT, WIDTH, C), first_grad, second_grad


def solution(mesh):
    placed = (
        P(("rep", "dom"), None, None, None),
        P(("rep", "dom"), None, None, None),
        P(("rep", "dom")),
        P(),
        P(),
        P("dom", None),
        P("dom", None),
    )
    return jax.shard_map(
        body,
        mesh=mesh,
        in_specs=placed,
        out_specs=(P(("rep", "dom"), None, None, None), P("dom", None), P("dom", None)),
        check_vma=False,
    )
```

```python
import math

import jax
import jax.numpy as jnp
from jax import lax
from jax.experimental import pallas as pl
from jax.experimental.pallas import tpu as pltpu
from jax.sharding import PartitionSpec as P

C = 320
TEMB = 1280
HEIGHT = 8
WIDTH = 16
PIX = HEIGHT * WIDTH
NX, NY, NZH, NZL = 4, 4, 4, 8
BLOCK = 180
QROWS = 48
SAMPLES = 1024
MESH = pl.DeviceIdType.MESH
norm_eps = 1e-05
bf16 = jnp.bfloat16
f32 = jnp.float32

VM = pl.BlockSpec(memory_space=pltpu.VMEM)
SM = pl.BlockSpec(memory_space=pltpu.SMEM)


def position():
    rep, dom = lax.axis_index("rep"), lax.axis_index("dom")
    return rep // 8, lax.rem(rep // 2, 4), lax.rem(rep, 2), dom // 4, lax.rem(dom, 4)


def device(z_lo, x, core, z_hi, y):
    return {"rep": z_lo * 8 + x * 2 + core, "dom": z_hi * 4 + y}


def send(src, dst, send_sem, recv_sem, target):
    copy = pltpu.make_async_remote_copy(
        src_ref=src, dst_ref=dst, send_sem=send_sem, recv_sem=recv_sem,
        device_id=target, device_id_type=MESH,
    )
    copy.start()
    return copy


def group_matrix():
    row = lax.broadcasted_iota(jnp.int32, (C, C), 0).astype(f32)
    col = lax.broadcasted_iota(jnp.int32, (C, C), 1).astype(f32)
    same = jnp.floor((row + 0.5) * 0.1) == jnp.floor((col + 0.5) * 0.1)
    return jnp.where(same, 1.0, 0.0).astype(f32)


def shifted(v, step, rows):
    if step == 0:
        return v
    column = lax.rem(lax.broadcasted_iota(jnp.int32, (rows, C), 0), WIDTH)
    inside = (column + step >= 0) & (column + step < WIDTH)
    return jnp.where(inside, pltpu.roll(v, (-step) % rows, 0), 0.0)


def pack_block(w):
    w = w.astype(f32)
    pad = jnp.zeros((12, 128), f32)
    fold = jnp.concatenate(
        [w[0:96, 256:320], jnp.concatenate([w[96:180, 256:320], jnp.zeros((12, 64), f32)], axis=0)], axis=1
    )
    tiles = jnp.concatenate([w[:, 0:128], pad, w[:, 128:256], pad, fold, jnp.zeros((32, 128), f32)], axis=0)
    return tiles.astype(bf16).reshape(4, 128, 128)


def gather_weights(c, own, wg, keep, other, to_z, to_x, to_y, place, extra, zs, zr, so, ro, s2, r2, s3, r3, sc, rc):
    x, z_hi, y = place
    sent = []

    def go(*copy):
        sent.append(send(*copy))
        return sent[-1]

    def arrived(copies):
        for copy in copies:
            copy.wait_recv()

    def block(d):
        return lax.rem(z_hi + 4 - d, 4)

    zc = {
        d: go(own.at[c, x], wg.at[c, z_hi * 4 + y, x], zs.at[d - 1], zr.at[d - 1], to_z[d - 1])
        for d in (2, 1, 3)
    }
    oc = [go(own.at[c], wg.at[c, z_hi * 4 + y], so.at[j], ro.at[j], to_y[j]) for j in (1, 0, 2)]
    extra(go)
    near, far = (to_x, to_y) if c == 0 else (to_y, to_x)

    def second(d):
        arrived([zc[d]])
        part = wg.at[c, block(d) * 4 + y, x]
        return [go(part, part, s2.at[d - 1, j], r2.at[d - 1, j], near[j]) for j in (1, 0, 2)]

    def third(d, before):
        arrived(before)
        if c == 0:
            part = wg.at[0, block(d) * 4 + y]
            return [go(part, part, s3.at[d - 1, 0, j], r3.at[d - 1, 0, j], far[j]) for j in (1, 0, 2)]
        copies = []
        for i in range(4):
            part = wg.at[1, block(d) * 4 + lax.rem(y + i, 4), x]
            copies += [go(part, part, s3.at[d - 1, i, j], r3.at[d - 1, i, j], far[j]) for j in (1, 0, 2)]
        return copies

    def fourth(d, before):
        arrived(before)
        part = wg.at[c, pl.ds(block(d) * 4, 4)]
        return [go(part, part, sc.at[d], rc.at[d], other)]

    for copy in keep:
        copy.wait()
    a1 = second(1)
    a3 = second(3)
    b1 = third(1, a1)
    b3 = third(3, a3)
    arrived(oc)
    last = []
    for i in (1, 2, 3):
        part = wg.at[c, z_hi * 4 + lax.rem(y + i, 4)]
        last.append(go(part, part, sc.at[3 + i], rc.at[3 + i], other))
    a2 = second(2)
    last += fourth(1, b1)
    b2 = third(2, a2)
    last += fourth(3, b3)
    last += fourth(2, b2)
    arrived(last)
    for copy in sent:
        copy.wait_send()


def step_kernel(
    index_ref, tile_ref, odd_ref, x_ref, cot_ref, bias_ref, w1_ref, w2_ref,
    out_ref, all_ref,
    own, wg, wl1, wl2, pad, act1, act2, cgrad, acts, grads, act_t, pads, total,
    part_ref, ybuf, s1, zbuf, s2b, hbuf, final,
    own_sem, zs, zr, so, ro, s2, r2, s3, r3, sc, rc, sa, ra,
    ys, yr, ls, lr, hs, hr, gs, gr, xs, xr, cs, cr, keep_sem,
):
    z_lo, x, core, z_hi, y = position()
    slot = x * 2 + core
    to_z = [device(z_lo, x, core, lax.rem(z_hi + d, 4), y) for d in (1, 2, 3)]
    to_y = [device(z_lo, x, core, z_hi, lax.rem(y + d, 4)) for d in (1, 2, 3)]
    to_l = [device(lax.rem(z_lo + d, 8), x, core, z_hi, y) for d in range(1, 8)]
    at_x = [[device(z_lo, lax.rem(x + d, 4), c, z_hi, y) for d in (1, 2, 3)] for c in (0, 1)]
    to_x = [device(z_lo, lax.rem(x + d, 4), core, z_hi, y) for d in (1, 2, 3)]
    other = device(z_lo, x, 1 - core, z_hi, y)
    partners = to_z + to_y + to_l + at_x[0] + at_x[1] + [other]
    barrier = pltpu.get_barrier_semaphore()
    for partner in partners:
        pl.semaphore_signal(barrier, inc=1, device_id=partner, device_id_type=MESH)

    member = group_matrix()
    count = 1.0 / (PIX * 10)

    def group_mean(v):
        column = jnp.sum(v, axis=0, keepdims=True)
        return jnp.dot(
            jnp.broadcast_to(column, (8, C)), member,
            precision=lax.Precision.HIGHEST, preferred_element_type=f32,
        )[0:1] * count

    def group_norm(v):
        centered = v - group_mean(v)
        inverse_std = lax.rsqrt(group_mean(centered * centered) + norm_eps)
        return centered * inverse_std, inverse_std

    own[0] = pack_block(w1_ref[...])
    own[1] = pack_block(w2_ref[...])
    source = x_ref[...].astype(f32)
    normed, _ = group_norm(source)
    act1[...] = (normed * (1.0 / (1.0 + jnp.exp(-normed)))).astype(bf16)
    pad[:, 0:16, :] = jnp.zeros((3, 16, C), bf16)
    pad[:, 144:160, :] = jnp.zeros((3, 16, C), bf16)
    pads[:, :, 0:16, :] = jnp.zeros((3, 8, 16, C), bf16)
    pads[:, :, 144:160, :] = jnp.zeros((3, 8, 16, C), bf16)
    total[9 * C // 8 :] = jnp.zeros((3, 8, C), f32)

    def fill(v):
        for k in range(3):
            pad[k, 16:144, :] = shifted(v, k - 1, PIX).astype(bf16)

    fill(act1[...].astype(f32))

    @pl.when(core == 0)
    def _():
        acts[slot] = act1[...]

    @pl.when(core == 1)
    def _():
        grads[slot] = cot_ref[...]

    pl.semaphore_wait(barrier, len(partners))

    keep = [pltpu.make_async_copy(own.at[k], wg.at[k, z_hi * 4 + y], own_sem.at[k]) for k in (0, 1)]
    for copy in keep:
        copy.start()

    for c in (0, 1):

        def run(c=c):
            def extra(go):
                for j in (1, 0, 2):
                    go(act1, acts.at[slot], sa.at[0, j + 1], ra.at[0, j + 1, c], at_x[0][j])
                    go(cot_ref, grads.at[slot], sa.at[2, j + 1], ra.at[1, j + 1, c], at_x[1][j])
                if c == 1:
                    go(act1, acts.at[slot], sa.at[0, 0], ra.at[0, 0, 1], other)
                else:
                    go(cot_ref, grads.at[slot], sa.at[2, 0], ra.at[1, 0, 0], other)

            gather_weights(
                c, own, wg, keep, other, to_z, to_x, to_y, (x, z_hi, y), extra,
                zs, zr, so, ro, s2, r2, s3, r3, sc, rc,
            )

        pl.when(core == c)(run)

    for kernel, target in ((0, wl1), (1, wl2)):
        for j in range(16):
            v = wg[kernel, index_ref[j]].reshape(512, 128)
            base = BLOCK * j
            target[base : base + 180, 0:128] = v[0:180]
            target[base : base + 180, 128:256] = v[192:372]
            target[base : base + 96, 256:320] = v[384:480, 0:64]
            target[base + 96 : base + 180, 256:320] = v[384:468, 64:128]

    def conv(weight):
        result = jnp.zeros((PIX, C), f32)
        for t in range(9):
            ky, kx = t // 3, t % 3
            result = result + jnp.dot(
                pad[kx, 16 * ky : 16 * ky + PIX, :], weight[C * t : C * t + C, :],
                preferred_element_type=f32,
            )
        return result

    second_norm, second_std = group_norm(conv(wl1) + bias_ref[...])
    gate = 1.0 / (1.0 + jnp.exp(-second_norm))
    second_act = (second_norm * gate).astype(bf16)
    act2[...] = second_act

    @pl.when(core == 1)
    def _():
        acts[slot] = act2[...]

    fill(cot_ref[...].astype(f32))
    sent = [
        send(act2, acts.at[slot], sa.at[1, j + 1], ra.at[0, j + 1, core], at_x[1][j]) for j in (1, 0, 2)
    ]

    @pl.when(core == 0)
    def _():
        send(act2, acts.at[slot], sa.at[1, 0], ra.at[0, 0, 0], other)

    act_grad = jnp.zeros((PIX, C), f32)
    for t in range(9):
        ky, kx = 2 - t // 3, 2 - t % 3
        act_grad = act_grad + lax.dot_general(
            pad[kx, 16 * ky : 16 * ky + PIX, :], wl2[C * t : C * t + C, :],
            (((1,), (1,)), ((), ())), preferred_element_type=f32,
        )
    norm_grad = act_grad * gate * (1.0 + second_norm * (1.0 - gate))
    cgrad[...] = (
        second_std
        * (norm_grad - group_mean(norm_grad) - second_norm * group_mean(norm_grad * second_norm))
    ).astype(bf16)

    @pl.when(core == 0)
    def _():
        grads[slot] = cgrad[...]

    sent += [
        send(cgrad, grads.at[slot], sa.at[3, j + 1], ra.at[1, j + 1, core], at_x[0][j]) for j in (1, 0, 2)
    ]

    @pl.when(core == 1)
    def _():
        send(cgrad, grads.at[slot], sa.at[3, 0], ra.at[1, 0, 1], other)

    fill(act2[...].astype(f32))
    out_ref[...] = (x_ref[...].astype(f32) + conv(wl2)).astype(bf16)

    def take_acts():
        for d in (1, 2, 3):
            for c in (0, 1):
                pltpu.make_async_copy(acts.at[slot], acts.at[slot], ra.at[0, d, c]).wait()
        pltpu.make_async_copy(acts.at[slot], acts.at[slot], ra.at[0, 0, 1 - core]).wait()

        @pl.loop(0, 8)
        def _(s):
            act_t[:, pl.ds(pl.multiple_of(PIX * s, PIX), PIX)] = acts[s].astype(f32).T.astype(bf16)

    def take_grads():
        for d in (1, 2, 3):
            for c in (0, 1):
                pltpu.make_async_copy(grads.at[slot], grads.at[slot], ra.at[1, d, c]).wait()
        pltpu.make_async_copy(grads.at[slot], grads.at[slot], ra.at[1, 0, 1 - core]).wait()

        @pl.loop(0, 8)
        def _(s):
            v = grads[s].astype(f32)
            for k in range(3):
                pads[k, s, 16:144, :] = shifted(v, k - 1, PIX).astype(bf16)

    @pl.when(core == 0)
    def _():
        take_acts()
        take_grads()
        pltpu.make_async_copy(act2, acts.at[slot], sa.at[1, 0]).wait()

    @pl.when(core == 1)
    def _():
        take_grads()
        take_acts()
        pltpu.make_async_copy(cgrad, grads.at[slot], sa.at[3, 0]).wait()

    for copy in sent:
        copy.wait_send()

    @pl.loop(0, 9)
    def _(t):
        ky, kx = 2 - t // 3, 2 - lax.rem(t, 3)
        rows = pads[kx, :, pl.ds(pl.multiple_of(16 * ky, 16), PIX), :].reshape(8 * PIX, C)
        product = jnp.dot(act_t[...], rows, preferred_element_type=f32)
        total[pl.ds((C // 8) * t, C // 8)] = product.reshape(C // 8, 8, C)

    ycopies = []
    for d in (2, 1, 3, 0):
        column = lax.rem(y + d, 4)
        for e in range(4):
            first = tile_ref[e * 4 + column]
            v = jnp.concatenate([total[first + i] for i in range(7)], axis=0)
            late = jnp.full((48, C), odd_ref[e * 4 + column], jnp.int32) > 0
            v = jnp.where(late, v[4:52], v[0:48])
            fold = jnp.concatenate([v[0:24, 256:320], v[24:48, 256:320]], axis=1)
            tile = jnp.concatenate([v[0:48, 0:128], v[0:48, 128:256], fold, jnp.zeros((8, 128), f32)], axis=0)
            part_ref[column, e] = tile.astype(bf16).reshape(NZL, 16, 128)
        if d > 0:
            ycopies.append(
                send(part_ref.at[column], ybuf.at[d - 1], ys.at[d - 1], yr.at[d - 1], to_y[d - 1])
            )
    for c in ycopies:
        c.wait()
    for e in range(NZH):
        v = part_ref[y, e].astype(f32)
        for d in range(3):
            v = v + ybuf[d, e].astype(f32)
        s1[:, e] = v.astype(bf16)

    copies = [
        send(s1.at[lax.rem(z_lo + d, 8)], zbuf.at[d - 1], ls.at[d - 1], lr.at[d - 1], to_l[d - 1])
        for d in (4, 3, 5, 2, 6, 1, 7)
    ]
    for c in copies:
        c.wait()
    v = s1[z_lo].astype(f32)
    for d in range(7):
        v = v + zbuf[d].astype(f32)
    s2b[...] = v.astype(bf16)

    copies = [
        send(s2b.at[lax.rem(z_hi + d, 4)], hbuf.at[d - 1], hs.at[d - 1], hr.at[d - 1], to_z[d - 1])
        for d in (2, 1, 3)
    ]
    for c in copies:
        c.wait()
    v = s2b[z_hi].astype(f32)
    for d in range(3):
        v = v + hbuf[d].astype(f32)
    final[...] = (v * (1.0 / SAMPLES)).astype(bf16)

    kept = pltpu.make_async_copy(final, all_ref.at[core, x, z_lo], keep_sem)
    kept.start()
    copies = [
        send(final, all_ref.at[core, x, z_lo], gs.at[d - 1], gr.at[d - 1], to_l[d - 1])
        for d in (4, 3, 5, 2, 6, 1, 7)
    ]
    kept.wait()
    for c in copies:
        c.wait()
    quarter = all_ref.at[core, x]
    copies = [send(quarter, quarter, xs.at[d - 1], xr.at[d - 1], to_x[d - 1]) for d in (2, 1, 3)]
    for c in copies:
        c.wait()
    whole = all_ref.at[core]
    send(whole, whole, cs, cr, other).wait()


def run_step(index, tiles, odd, x, cot, bias, first_weight, second_weight):
    dma = pltpu.SemaphoreType.DMA
    v = pltpu.VMEM
    return pl.pallas_call(
        step_kernel,
        out_shape=(
            jax.ShapeDtypeStruct((PIX, C), bf16),
            jax.ShapeDtypeStruct((2, NX, NZL, 16, 128), bf16),
        ),
        in_specs=[SM, SM, SM, VM, VM, VM, VM, VM],
        out_specs=(VM, VM),
        scratch_shapes=[
            v((2, 4, 128, 128), bf16), v((2, NZH * NY, 4, 128, 128), bf16),
            v((9 * C, C), bf16), v((9 * C, C), bf16), v((3, 160, C), bf16),
            v((PIX, C), bf16), v((PIX, C), bf16), v((PIX, C), bf16),
            v((8, PIX, C), bf16), v((8, PIX, C), bf16), v((C, 8 * PIX), bf16),
            v((3, 8, 160, C), bf16), v((9 * C // 8 + 3, 8, C), f32),
            v((NY, NZH, NZL, 16, 128), bf16), v((3, NZH, NZL, 16, 128), bf16),
            v((NZL, NZH, 16, 128), bf16), v((7, NZH, 16, 128), bf16), v((NZH, 16, 128), bf16),
            v((3, 16, 128), bf16), v((16, 128), bf16),
            dma((2,)), dma((3,)), dma((3,)), dma((3,)), dma((3,)), dma((3, 3)), dma((3, 3)),
            dma((3, 4, 3)), dma((3, 4, 3)), dma((7,)), dma((7,)), dma((4, 4)), dma((2, 4, 2)),
            dma((3,)), dma((3,)), dma((7,)), dma((7,)), dma((3,)), dma((3,)),
            dma((7,)), dma((7,)), dma((3,)), dma((3,)), dma, dma, dma,
        ],
        compiler_params=pltpu.CompilerParams(collective_id=0, has_side_effects=True),
        name="step",
    )(index, tiles, odd, x, cot, bias, first_weight, second_weight)


def finish_kernel(out_ref, all_ref, result_ref, first_ref, second_ref):
    result_ref[...] = out_ref[...]
    for kernel, target in ((0, first_ref), (1, second_ref)):
        for q in range(4):
            v = all_ref[kernel, q].astype(f32).reshape(128, 128)
            base, n = QROWS * q, min(QROWS, BLOCK - QROWS * q)
            target[base : base + n, 0:128] = v[0:n]
            target[base : base + n, 128:256] = v[48 : 48 + n]
            target[base : base + 24, 256:320] = v[96:120, 0:64]
            target[base + 24 : base + n, 256:320] = v[96 : 72 + n, 64:128]


def finish(out, everything):
    grad = jax.ShapeDtypeStruct((BLOCK, C), f32)
    return pl.pallas_call(
        finish_kernel,
        out_shape=(jax.ShapeDtypeStruct((PIX, C), bf16), grad, grad),
        in_specs=[VM, VM],
        out_specs=(VM, VM, VM),
        name="finish",
    )(out, everything)


def time_bias(timestep, time_weight):
    half_dim = TEMB // 2
    frequency = jnp.exp(-math.log(10000.0) * jnp.arange(half_dim, dtype=f32) / half_dim)
    angles = timestep.astype(f32) * frequency
    embedded = jnp.concatenate([jnp.cos(angles), jnp.sin(angles)])
    activated = jax.nn.silu(embedded).astype(bf16)
    return jnp.dot(activated[None, :], time_weight, preferred_element_type=f32)


def body(block_input, cotangent, timesteps, owner_map, time_weight, first_weight, second_weight):
    ids = jnp.arange(16, dtype=jnp.int32)
    inverse = jnp.sum((owner_map[None, :] == ids[:, None]).astype(jnp.int32) * ids[None, :], axis=1)
    quarter = lax.rem(lax.axis_index("rep") // 2, 4)
    starts = inverse * BLOCK + quarter.astype(jnp.int32) * QROWS
    bias = time_bias(timesteps[0], time_weight)
    x = block_input.reshape(PIX, C)
    cot = cotangent.reshape(PIX, C)
    out, everything = run_step(owner_map, starts // 8, lax.rem(starts // 4, 2), x, cot, bias, first_weight, second_weight)
    out, first_grad, second_grad = finish(out, everything)
    return out.reshape(1, HEIGHT, WIDTH, C), first_grad, second_grad


def solution(mesh):
    placed = (
        P(("rep", "dom"), None, None, None),
        P(("rep", "dom"), None, None, None),
        P(("rep", "dom")),
        P(),
        P(),
        P("dom", None),
        P("dom", None),
    )
    return jax.shard_map(
        body,
        mesh=mesh,
        in_specs=placed,
        out_specs=(P(("rep", "dom"), None, None, None), P("dom", None), P("dom", None)),
        check_vma=False,
    )
```

```python
import math

import jax
import jax.numpy as jnp
from jax import lax
from jax.experimental import pallas as pl
from jax.experimental.pallas import tpu as pltpu
from jax.sharding import PartitionSpec as P

C = 320
TEMB = 1280
HEIGHT = 8
WIDTH = 16
PIX = HEIGHT * WIDTH
NX, NY, NZH, NZL = 4, 4, 4, 8
BLOCK = 180
QROWS = 48
SAMPLES = 1024
MESH = pl.DeviceIdType.MESH
norm_eps = 1e-05
bf16 = jnp.bfloat16
f32 = jnp.float32

VM = pl.BlockSpec(memory_space=pltpu.VMEM)
SM = pl.BlockSpec(memory_space=pltpu.SMEM)


def position():
    rep, dom = lax.axis_index("rep"), lax.axis_index("dom")
    return rep // 8, lax.rem(rep // 2, 4), lax.rem(rep, 2), dom // 4, lax.rem(dom, 4)


def device(z_lo, x, core, z_hi, y):
    return {"rep": z_lo * 8 + x * 2 + core, "dom": z_hi * 4 + y}


def send(src, dst, send_sem, recv_sem, target):
    copy = pltpu.make_async_remote_copy(
        src_ref=src, dst_ref=dst, send_sem=send_sem, recv_sem=recv_sem,
        device_id=target, device_id_type=MESH,
    )
    copy.start()
    return copy


def group_matrix():
    row = lax.broadcasted_iota(jnp.int32, (C, C), 0).astype(f32)
    col = lax.broadcasted_iota(jnp.int32, (C, C), 1).astype(f32)
    same = jnp.floor((row + 0.5) * 0.1) == jnp.floor((col + 0.5) * 0.1)
    return jnp.where(same, 1.0, 0.0).astype(f32)


def shifted(v, step, rows):
    if step == 0:
        return v
    column = lax.rem(lax.broadcasted_iota(jnp.int32, (rows, C), 0), WIDTH)
    inside = (column + step >= 0) & (column + step < WIDTH)
    return jnp.where(inside, pltpu.roll(v, (-step) % rows, 0), 0.0)


def pack_block(w):
    w = w.astype(f32)
    pad = jnp.zeros((12, 128), f32)
    fold = jnp.concatenate(
        [w[0:96, 256:320], jnp.concatenate([w[96:180, 256:320], jnp.zeros((12, 64), f32)], axis=0)], axis=1
    )
    tiles = jnp.concatenate([w[:, 0:128], pad, w[:, 128:256], pad, fold, jnp.zeros((32, 128), f32)], axis=0)
    return tiles.astype(bf16).reshape(4, 2, 64, 128)


def gather_weights(c, own, wg, keep, other, to_z, to_x, to_y, place, extra, zs, zr, fs, fr, so, ro, s2, r2, s3, r3, sc, rc):
    x, z_hi, y = place
    sent = []

    def go(*copy):
        sent.append(send(*copy))
        return sent[-1]

    def arrived(copies):
        for copy in copies:
            copy.wait_recv()

    def block(d):
        return lax.rem(z_hi + 4 - d, 4)

    zc = {
        (d, h): go(own.at[c, x, h], wg.at[c, z_hi * 4 + y, x, h], zs.at[d - 1, h], zr.at[d - 1, h], to_z[d - 1])
        for d, h in ((1, 1), (3, 0), (1, 0), (3, 1))
    }
    oc = [go(own.at[c], wg.at[c, z_hi * 4 + y], so.at[j], ro.at[j], to_y[j]) for j in (1, 0, 2)]
    extra(go)
    near, far = (to_x, to_y) if c == 0 else (to_y, to_x)

    def relay(d, h):
        arrived([zc[d, h]])
        part = wg.at[c, block(d) * 4 + y, x, h]
        return go(part, part, fs.at[h], fr.at[h], to_z[d - 1])

    def second(d, before):
        arrived(before)
        part = wg.at[c, block(d) * 4 + y, x]
        return [go(part, part, s2.at[d - 1, j], r2.at[d - 1, j], near[j]) for j in (1, 0, 2)]

    def third(d, before):
        arrived(before)
        if c == 0:
            part = wg.at[0, block(d) * 4 + y]
            return [go(part, part, s3.at[d - 1, 0, j], r3.at[d - 1, 0, j], far[j]) for j in (1, 0, 2)]
        copies = []
        for i in range(4):
            part = wg.at[1, block(d) * 4 + lax.rem(y + i, 4), x]
            copies += [go(part, part, s3.at[d - 1, i, j], r3.at[d - 1, i, j], far[j]) for j in (1, 0, 2)]
        return copies

    def fourth(d, before):
        arrived(before)
        part = wg.at[c, pl.ds(block(d) * 4, 4)]
        return [go(part, part, sc.at[d], rc.at[d], other)]

    for copy in keep:
        copy.wait()
    upper = relay(1, 1)
    lower = relay(3, 0)
    a1 = second(1, [zc[1, 0]])
    a3 = second(3, [zc[3, 1]])
    b1 = third(1, a1)
    b3 = third(3, a3)
    arrived(oc)
    last = []
    for i in (1, 2, 3):
        part = wg.at[c, z_hi * 4 + lax.rem(y + i, 4)]
        last.append(go(part, part, sc.at[3 + i], rc.at[3 + i], other))
    a2 = second(2, [upper, lower])
    last += fourth(1, b1)
    b2 = third(2, a2)
    last += fourth(3, b3)
    last += fourth(2, b2)
    arrived(last)
    for copy in sent:
        copy.wait_send()


def step_kernel(
    index_ref, tile_ref, odd_ref, x_ref, cot_ref, bias_ref, w1_ref, w2_ref,
    out_ref, all_ref,
    own, wg, wl1, wl2, pad, act1, act2, cgrad, acts, grads, act_t, pads, total,
    part_ref, ybuf, s1, zbuf, s2b, hbuf, final,
    own_sem, zs, zr, fs, fr, so, ro, s2, r2, s3, r3, sc, rc, sa, ra,
    ys, yr, ls, lr, hs, hr, gs, gr, xs, xr, cs, cr, keep_sem,
):
    z_lo, x, core, z_hi, y = position()
    slot = x * 2 + core
    to_z = [device(z_lo, x, core, lax.rem(z_hi + d, 4), y) for d in (1, 2, 3)]
    to_y = [device(z_lo, x, core, z_hi, lax.rem(y + d, 4)) for d in (1, 2, 3)]
    to_l = [device(lax.rem(z_lo + d, 8), x, core, z_hi, y) for d in range(1, 8)]
    at_x = [[device(z_lo, lax.rem(x + d, 4), c, z_hi, y) for d in (1, 2, 3)] for c in (0, 1)]
    to_x = [device(z_lo, lax.rem(x + d, 4), core, z_hi, y) for d in (1, 2, 3)]
    other = device(z_lo, x, 1 - core, z_hi, y)
    partners = to_z + to_y + to_l + at_x[0] + at_x[1] + [other]
    barrier = pltpu.get_barrier_semaphore()
    for partner in partners:
        pl.semaphore_signal(barrier, inc=1, device_id=partner, device_id_type=MESH)

    member = group_matrix()
    count = 1.0 / (PIX * 10)

    def group_mean(v):
        column = jnp.sum(v, axis=0, keepdims=True)
        return jnp.dot(
            jnp.broadcast_to(column, (8, C)), member,
            precision=lax.Precision.HIGHEST, preferred_element_type=f32,
        )[0:1] * count

    def group_norm(v):
        centered = v - group_mean(v)
        inverse_std = lax.rsqrt(group_mean(centered * centered) + norm_eps)
        return centered * inverse_std, inverse_std

    own[0] = pack_block(w1_ref[...])
    own[1] = pack_block(w2_ref[...])
    source = x_ref[...].astype(f32)
    normed, _ = group_norm(source)
    act1[...] = (normed * (1.0 / (1.0 + jnp.exp(-normed)))).astype(bf16)
    pad[:, 0:16, :] = jnp.zeros((3, 16, C), bf16)
    pad[:, 144:160, :] = jnp.zeros((3, 16, C), bf16)
    pads[:, :, 0:16, :] = jnp.zeros((3, 8, 16, C), bf16)
    pads[:, :, 144:160, :] = jnp.zeros((3, 8, 16, C), bf16)
    total[9 * C // 8 :] = jnp.zeros((3, 8, C), f32)

    def fill(v):
        for k in range(3):
            pad[k, 16:144, :] = shifted(v, k - 1, PIX).astype(bf16)

    fill(act1[...].astype(f32))

    @pl.when(core == 0)
    def _():
        acts[slot] = act1[...]

    @pl.when(core == 1)
    def _():
        grads[slot] = cot_ref[...]

    pl.semaphore_wait(barrier, len(partners))

    keep = [pltpu.make_async_copy(own.at[k], wg.at[k, z_hi * 4 + y], own_sem.at[k]) for k in (0, 1)]
    for copy in keep:
        copy.start()

    for c in (0, 1):

        def run(c=c):
            def extra(go):
                for j in (1, 0, 2):
                    go(act1, acts.at[slot], sa.at[0, j + 1], ra.at[0, j + 1, c], at_x[0][j])
                    go(cot_ref, grads.at[slot], sa.at[2, j + 1], ra.at[1, j + 1, c], at_x[1][j])
                if c == 1:
                    go(act1, acts.at[slot], sa.at[0, 0], ra.at[0, 0, 1], other)
                else:
                    go(cot_ref, grads.at[slot], sa.at[2, 0], ra.at[1, 0, 0], other)

            gather_weights(
                c, own, wg, keep, other, to_z, to_x, to_y, (x, z_hi, y), extra,
                zs, zr, fs, fr, so, ro, s2, r2, s3, r3, sc, rc,
            )

        pl.when(core == c)(run)

    for kernel, target in ((0, wl1), (1, wl2)):
        for j in range(16):
            v = wg[kernel, index_ref[j]].reshape(512, 128)
            base = BLOCK * j
            target[base : base + 180, 0:128] = v[0:180]
            target[base : base + 180, 128:256] = v[192:372]
            target[base : base + 96, 256:320] = v[384:480, 0:64]
            target[base + 96 : base + 180, 256:320] = v[384:468, 64:128]

    def conv(weight):
        result = jnp.zeros((PIX, C), f32)
        for t in range(9):
            ky, kx = t // 3, t % 3
            result = result + jnp.dot(
                pad[kx, 16 * ky : 16 * ky + PIX, :], weight[C * t : C * t + C, :],
                preferred_element_type=f32,
            )
        return result

    second_norm, second_std = group_norm(conv(wl1) + bias_ref[...])
    gate = 1.0 / (1.0 + jnp.exp(-second_norm))
    second_act = (second_norm * gate).astype(bf16)
    act2[...] = second_act

    @pl.when(core == 1)
    def _():
        acts[slot] = act2[...]

    fill(cot_ref[...].astype(f32))
    sent = [
        send(act2, acts.at[slot], sa.at[1, j + 1], ra.at[0, j + 1, core], at_x[1][j]) for j in (1, 0, 2)
    ]

    @pl.when(core == 0)
    def _():
        send(act2, acts.at[slot], sa.at[1, 0], ra.at[0, 0, 0], other)

    act_grad = jnp.zeros((PIX, C), f32)
    for t in range(9):
        ky, kx = 2 - t // 3, 2 - t % 3
        act_grad = act_grad + lax.dot_general(
            pad[kx, 16 * ky : 16 * ky + PIX, :], wl2[C * t : C * t + C, :],
            (((1,), (1,)), ((), ())), preferred_element_type=f32,
        )
    norm_grad = act_grad * gate * (1.0 + second_norm * (1.0 - gate))
    cgrad[...] = (
        second_std
        * (norm_grad - group_mean(norm_grad) - second_norm * group_mean(norm_grad * second_norm))
    ).astype(bf16)

    @pl.when(core == 0)
    def _():
        grads[slot] = cgrad[...]

    sent += [
        send(cgrad, grads.at[slot], sa.at[3, j + 1], ra.at[1, j + 1, core], at_x[0][j]) for j in (1, 0, 2)
    ]

    @pl.when(core == 1)
    def _():
        send(cgrad, grads.at[slot], sa.at[3, 0], ra.at[1, 0, 1], other)

    fill(act2[...].astype(f32))
    out_ref[...] = (x_ref[...].astype(f32) + conv(wl2)).astype(bf16)

    def take_acts():
        for d in (1, 2, 3):
            for c in (0, 1):
                pltpu.make_async_copy(acts.at[slot], acts.at[slot], ra.at[0, d, c]).wait()
        pltpu.make_async_copy(acts.at[slot], acts.at[slot], ra.at[0, 0, 1 - core]).wait()

        @pl.loop(0, 8)
        def _(s):
            act_t[:, pl.ds(pl.multiple_of(PIX * s, PIX), PIX)] = acts[s].astype(f32).T.astype(bf16)

    def take_grads():
        for d in (1, 2, 3):
            for c in (0, 1):
                pltpu.make_async_copy(grads.at[slot], grads.at[slot], ra.at[1, d, c]).wait()
        pltpu.make_async_copy(grads.at[slot], grads.at[slot], ra.at[1, 0, 1 - core]).wait()

        @pl.loop(0, 8)
        def _(s):
            v = grads[s].astype(f32)
            for k in range(3):
                pads[k, s, 16:144, :] = shifted(v, k - 1, PIX).astype(bf16)

    @pl.when(core == 0)
    def _():
        take_acts()
        take_grads()
        pltpu.make_async_copy(act2, acts.at[slot], sa.at[1, 0]).wait()

    @pl.when(core == 1)
    def _():
        take_grads()
        take_acts()
        pltpu.make_async_copy(cgrad, grads.at[slot], sa.at[3, 0]).wait()

    for copy in sent:
        copy.wait_send()

    @pl.loop(0, 9)
    def _(t):
        ky, kx = 2 - t // 3, 2 - lax.rem(t, 3)
        rows = pads[kx, :, pl.ds(pl.multiple_of(16 * ky, 16), PIX), :].reshape(8 * PIX, C)
        product = jnp.dot(act_t[...], rows, preferred_element_type=f32)
        total[pl.ds((C // 8) * t, C // 8)] = product.reshape(C // 8, 8, C)

    steps = (2, 1, 3, 0)
    ycopies, lcopies, hcopies = [], [], []
    for i, step in enumerate(steps):
        holder = lax.rem(z_hi + step, 4)
        ycopies.append([])
        for d in (2, 1, 3, 0):
            column = lax.rem(y + d, 4)
            first = tile_ref[holder * 4 + column]
            v = jnp.concatenate([total[first + n] for n in range(7)], axis=0)
            late = jnp.full((48, C), odd_ref[holder * 4 + column], jnp.int32) > 0
            v = jnp.where(late, v[4:52], v[0:48])
            fold = jnp.concatenate([v[0:24, 256:320], v[24:48, 256:320]], axis=1)
            tile = jnp.concatenate([v[0:48, 0:128], v[0:48, 128:256], fold, jnp.zeros((8, 128), f32)], axis=0)
            part_ref[i, column] = tile.astype(bf16).reshape(NZL, 16, 128)
            if d > 0:
                ycopies[i].append(
                    send(part_ref.at[i, column], ybuf.at[d - 1, i], ys.at[d - 1, i], yr.at[d - 1, i], to_y[d - 1])
                )
    for i in range(4):
        for c in ycopies[i]:
            c.wait()
        v = part_ref[i, y].astype(f32)
        for d in range(3):
            v = v + ybuf[d, i].astype(f32)
        s1[i] = v.astype(bf16)
        lcopies.append([
            send(s1.at[i, lax.rem(z_lo + d, 8)], zbuf.at[d - 1, i], ls.at[d - 1, i], lr.at[d - 1, i], to_l[d - 1])
            for d in (4, 3, 5, 2, 6, 1, 7)
        ])
    for i, step in enumerate(steps):
        for c in lcopies[i]:
            c.wait()
        v = s1[i, z_lo].astype(f32)
        for d in range(7):
            v = v + zbuf[d, i].astype(f32)
        if step > 0:
            s2b[i] = v.astype(bf16)
            hcopies.append(send(s2b.at[i], hbuf.at[i], hs.at[i], hr.at[i], to_z[step - 1]))
    for i in (1, 2, 0):
        hcopies[i].wait()
        v = v + hbuf[i].astype(f32)
    final[...] = (v * (1.0 / SAMPLES)).astype(bf16)

    kept = pltpu.make_async_copy(final, all_ref.at[core, x, z_lo], keep_sem)
    kept.start()
    copies = [
        send(final, all_ref.at[core, x, z_lo], gs.at[d - 1], gr.at[d - 1], to_l[d - 1])
        for d in (4, 3, 5, 2, 6, 1, 7)
    ]
    kept.wait()
    for c in copies:
        c.wait()
    quarter = all_ref.at[core, x]
    copies = [send(quarter, quarter, xs.at[d - 1], xr.at[d - 1], to_x[d - 1]) for d in (2, 1, 3)]
    for c in copies:
        c.wait()
    whole = all_ref.at[core]
    send(whole, whole, cs, cr, other).wait()


def run_step(index, tiles, odd, x, cot, bias, first_weight, second_weight):
    dma = pltpu.SemaphoreType.DMA
    v = pltpu.VMEM
    return pl.pallas_call(
        step_kernel,
        out_shape=(
            jax.ShapeDtypeStruct((PIX, C), bf16),
            jax.ShapeDtypeStruct((2, NX, NZL, 16, 128), bf16),
        ),
        in_specs=[SM, SM, SM, VM, VM, VM, VM, VM],
        out_specs=(VM, VM),
        scratch_shapes=[
            v((2, 4, 2, 64, 128), bf16), v((2, NZH * NY, 4, 2, 64, 128), bf16),
            v((9 * C, C), bf16), v((9 * C, C), bf16), v((3, 160, C), bf16),
            v((PIX, C), bf16), v((PIX, C), bf16), v((PIX, C), bf16),
            v((8, PIX, C), bf16), v((8, PIX, C), bf16), v((C, 8 * PIX), bf16),
            v((3, 8, 160, C), bf16), v((9 * C // 8 + 3, 8, C), f32),
            v((NZH, NY, NZL, 16, 128), bf16), v((3, NZH, NZL, 16, 128), bf16),
            v((NZH, NZL, 16, 128), bf16), v((7, NZH, 16, 128), bf16), v((3, 16, 128), bf16),
            v((3, 16, 128), bf16), v((16, 128), bf16),
            dma((2,)), dma((3, 2)), dma((3, 2)), dma((2,)), dma((2,)), dma((3,)), dma((3,)), dma((3, 3)), dma((3, 3)),
            dma((3, 4, 3)), dma((3, 4, 3)), dma((7,)), dma((7,)), dma((4, 4)), dma((2, 4, 2)),
            dma((3, 4)), dma((3, 4)), dma((7, 4)), dma((7, 4)), dma((3,)), dma((3,)),
            dma((7,)), dma((7,)), dma((3,)), dma((3,)), dma, dma, dma,
        ],
        compiler_params=pltpu.CompilerParams(collective_id=0, has_side_effects=True),
        name="step",
    )(index, tiles, odd, x, cot, bias, first_weight, second_weight)


def finish_kernel(out_ref, all_ref, result_ref, first_ref, second_ref):
    result_ref[...] = out_ref[...]
    for kernel, target in ((0, first_ref), (1, second_ref)):
        for q in range(4):
            v = all_ref[kernel, q].astype(f32).reshape(128, 128)
            base, n = QROWS * q, min(QROWS, BLOCK - QROWS * q)
            target[base : base + n, 0:128] = v[0:n]
            target[base : base + n, 128:256] = v[48 : 48 + n]
            target[base : base + 24, 256:320] = v[96:120, 0:64]
            target[base + 24 : base + n, 256:320] = v[96 : 72 + n, 64:128]


def finish(out, everything):
    grad = jax.ShapeDtypeStruct((BLOCK, C), f32)
    return pl.pallas_call(
        finish_kernel,
        out_shape=(jax.ShapeDtypeStruct((PIX, C), bf16), grad, grad),
        in_specs=[VM, VM],
        out_specs=(VM, VM, VM),
        name="finish",
    )(out, everything)


def time_bias(timestep, time_weight):
    half_dim = TEMB // 2
    frequency = jnp.exp(-math.log(10000.0) * jnp.arange(half_dim, dtype=f32) / half_dim)
    angles = timestep.astype(f32) * frequency
    embedded = jnp.concatenate([jnp.cos(angles), jnp.sin(angles)])
    activated = jax.nn.silu(embedded).astype(bf16)
    return jnp.dot(activated[None, :], time_weight, preferred_element_type=f32)


def body(block_input, cotangent, timesteps, owner_map, time_weight, first_weight, second_weight):
    ids = jnp.arange(16, dtype=jnp.int32)
    inverse = jnp.sum((owner_map[None, :] == ids[:, None]).astype(jnp.int32) * ids[None, :], axis=1)
    quarter = lax.rem(lax.axis_index("rep") // 2, 4)
    starts = inverse * BLOCK + quarter.astype(jnp.int32) * QROWS
    bias = time_bias(timesteps[0], time_weight)
    x = block_input.reshape(PIX, C)
    cot = cotangent.reshape(PIX, C)
    out, everything = run_step(owner_map, starts // 8, lax.rem(starts // 4, 2), x, cot, bias, first_weight, second_weight)
    out, first_grad, second_grad = finish(out, everything)
    return out.reshape(1, HEIGHT, WIDTH, C), first_grad, second_grad


def solution(mesh):
    placed = (
        P(("rep", "dom"), None, None, None),
        P(("rep", "dom"), None, None, None),
        P(("rep", "dom")),
        P(),
        P(),
        P("dom", None),
        P("dom", None),
    )
    return jax.shard_map(
        body,
        mesh=mesh,
        in_specs=placed,
        out_specs=(P(("rep", "dom"), None, None, None), P("dom", None), P("dom", None)),
        check_vma=False,
    )
```

```python
import math

import jax
import jax.numpy as jnp
from jax import lax
from jax.experimental import pallas as pl
from jax.experimental.pallas import tpu as pltpu
from jax.sharding import PartitionSpec as P

C = 320
TEMB = 1280
HEIGHT = 8
WIDTH = 16
PIX = HEIGHT * WIDTH
NX, NY, NZH, NZL = 4, 4, 4, 8
BLOCK = 180
QROWS = 48
SAMPLES = 1024
MESH = pl.DeviceIdType.MESH
norm_eps = 1e-05
bf16 = jnp.bfloat16
f32 = jnp.float32

VM = pl.BlockSpec(memory_space=pltpu.VMEM)
SM = pl.BlockSpec(memory_space=pltpu.SMEM)


def position():
    rep, dom = lax.axis_index("rep"), lax.axis_index("dom")
    return rep // 8, lax.rem(rep // 2, 4), lax.rem(rep, 2), dom // 4, lax.rem(dom, 4)


def device(z_lo, x, core, z_hi, y):
    return {"rep": z_lo * 8 + x * 2 + core, "dom": z_hi * 4 + y}


def send(src, dst, send_sem, recv_sem, target):
    copy = pltpu.make_async_remote_copy(
        src_ref=src, dst_ref=dst, send_sem=send_sem, recv_sem=recv_sem,
        device_id=target, device_id_type=MESH,
    )
    copy.start()
    return copy


def group_matrix():
    row = lax.broadcasted_iota(jnp.int32, (C, C), 0).astype(f32)
    col = lax.broadcasted_iota(jnp.int32, (C, C), 1).astype(f32)
    same = jnp.floor((row + 0.5) * 0.1) == jnp.floor((col + 0.5) * 0.1)
    return jnp.where(same, 1.0, 0.0).astype(f32)


def shifted(v, step, rows):
    if step == 0:
        return v
    column = lax.rem(lax.broadcasted_iota(jnp.int32, (rows, C), 0), WIDTH)
    inside = (column + step >= 0) & (column + step < WIDTH)
    return jnp.where(inside, pltpu.roll(v, (-step) % rows, 0), 0.0)


def pack_block(w):
    w = w.astype(f32)
    pad = jnp.zeros((12, 128), f32)
    fold = jnp.concatenate(
        [w[0:96, 256:320], jnp.concatenate([w[96:180, 256:320], jnp.zeros((12, 64), f32)], axis=0)], axis=1
    )
    tiles = jnp.concatenate([w[:, 0:128], pad, w[:, 128:256], pad, fold, jnp.zeros((32, 128), f32)], axis=0)
    return tiles.astype(bf16).reshape(4, 2, 64, 128)


def gather_weights(c, own, wg, keep, other, to_z, to_x, to_y, place, extra, zs, zr, fs, fr, so, ro, s2, r2, s3, r3, sc, rc):
    x, z_hi, y = place
    sent = []

    def go(*copy):
        sent.append(send(*copy))
        return sent[-1]

    def arrived(copies):
        for copy in copies:
            copy.wait_recv()

    def block(d):
        return lax.rem(z_hi + 4 - d, 4)

    zc = {
        (d, h): go(own.at[c, x, h], wg.at[c, z_hi * 4 + y, x, h], zs.at[d - 1, h], zr.at[d - 1, h], to_z[d])
        for d, h in ((1, 1), (3, 0), (1, 0), (3, 1))
    }
    oc = [go(own.at[c], wg.at[c, z_hi * 4 + y], so.at[j], ro.at[j], to_y[j]) for j in (1, 0, 2)]
    extra(go)
    near, far = (to_x, to_y) if c == 0 else (to_y, to_x)

    def relay(d, h):
        arrived([zc[d, h]])
        part = wg.at[c, block(d) * 4 + y, x, h]
        return go(part, part, fs.at[h], fr.at[h], to_z[d])

    def second(d, before):
        arrived(before)
        part = wg.at[c, block(d) * 4 + y, x]
        return [go(part, part, s2.at[d - 1, j], r2.at[d - 1, j], near[j]) for j in (1, 0, 2)]

    def third(d, before):
        arrived(before)
        if c == 0:
            part = wg.at[0, block(d) * 4 + y]
            return [go(part, part, s3.at[d - 1, 0, j], r3.at[d - 1, 0, j], far[j]) for j in (1, 0, 2)]
        copies = []
        for i in range(4):
            part = wg.at[1, block(d) * 4 + lax.rem(y + i, 4), x]
            copies += [go(part, part, s3.at[d - 1, i, j], r3.at[d - 1, i, j], far[j]) for j in (1, 0, 2)]
        return copies

    def fourth(d, before):
        arrived(before)
        part = wg.at[c, pl.ds(block(d) * 4, 4)]
        return [go(part, part, sc.at[d], rc.at[d], other)]

    for copy in keep:
        copy.wait()
    upper = relay(1, 1)
    lower = relay(3, 0)
    a1 = second(1, [zc[1, 0]])
    a3 = second(3, [zc[3, 1]])
    b1 = third(1, a1)
    b3 = third(3, a3)
    arrived(oc)
    last = []
    for i in (1, 2, 3):
        part = wg.at[c, z_hi * 4 + lax.rem(y + i, 4)]
        last.append(go(part, part, sc.at[3 + i], rc.at[3 + i], other))
    a2 = second(2, [upper, lower])
    last += fourth(1, b1)
    b2 = third(2, a2)
    last += fourth(3, b3)
    last += fourth(2, b2)
    arrived(last)
    for copy in sent:
        copy.wait_send()


def step_kernel(
    index_ref, tile_ref, odd_ref, x_ref, cot_ref, bias_ref, w1_ref, w2_ref,
    out_ref, all_ref,
    own, wg, wl1, wl2, pad, act1, act2, cgrad, acts, grads, act_t, pads, total,
    part_ref, ybuf, s1, zbuf, s2b, hbuf, final,
    own_sem, zs, zr, fs, fr, so, ro, s2, r2, s3, r3, sc, rc, sa, ra,
    ys, yr, ls, lr, hs, hr, gs, gr, xs, xr, cs, cr, keep_sem,
):
    z_lo, x, core, z_hi, y = position()
    slot = x * 2 + core
    to_z = {d: device(z_lo, x, core, lax.rem(z_hi + d, 4), y) for d in (1, 3)}
    to_y = [device(z_lo, x, core, z_hi, lax.rem(y + d, 4)) for d in (1, 2, 3)]
    to_l = [device(lax.rem(z_lo + d, 8), x, core, z_hi, y) for d in range(1, 8)]
    at_x = [[device(z_lo, lax.rem(x + d, 4), c, z_hi, y) for d in (1, 2, 3)] for c in (0, 1)]
    to_x = [device(z_lo, lax.rem(x + d, 4), core, z_hi, y) for d in (1, 2, 3)]
    other = device(z_lo, x, 1 - core, z_hi, y)
    partners = [to_z[1], to_z[3]] + to_y + to_l + at_x[0] + at_x[1] + [other]
    barrier = pltpu.get_barrier_semaphore()
    for partner in partners:
        pl.semaphore_signal(barrier, inc=1, device_id=partner, device_id_type=MESH)

    member = group_matrix()
    count = 1.0 / (PIX * 10)

    def group_mean(v):
        column = jnp.sum(v, axis=0, keepdims=True)
        return jnp.dot(
            jnp.broadcast_to(column, (8, C)), member,
            precision=lax.Precision.HIGHEST, preferred_element_type=f32,
        )[0:1] * count

    def group_norm(v):
        centered = v - group_mean(v)
        inverse_std = lax.rsqrt(group_mean(centered * centered) + norm_eps)
        return centered * inverse_std, inverse_std

    own[0] = pack_block(w1_ref[...])
    own[1] = pack_block(w2_ref[...])
    source = x_ref[...].astype(f32)
    normed, _ = group_norm(source)
    act1[...] = (normed * (1.0 / (1.0 + jnp.exp(-normed)))).astype(bf16)
    pad[:, 0:16, :] = jnp.zeros((3, 16, C), bf16)
    pad[:, 144:160, :] = jnp.zeros((3, 16, C), bf16)
    pads[:, :, 0:16, :] = jnp.zeros((3, 8, 16, C), bf16)
    pads[:, :, 144:160, :] = jnp.zeros((3, 8, 16, C), bf16)
    total[9 * C // 8 :] = jnp.zeros((3, 8, C), f32)

    def fill(v):
        for k in range(3):
            pad[k, 16:144, :] = shifted(v, k - 1, PIX).astype(bf16)

    fill(act1[...].astype(f32))

    @pl.when(core == 0)
    def _():
        acts[slot] = act1[...]

    @pl.when(core == 1)
    def _():
        grads[slot] = cot_ref[...]

    pl.semaphore_wait(barrier, len(partners))

    keep = [pltpu.make_async_copy(own.at[k], wg.at[k, z_hi * 4 + y], own_sem.at[k]) for k in (0, 1)]
    for copy in keep:
        copy.start()

    for c in (0, 1):

        def run(c=c):
            def extra(go):
                for j in (1, 0, 2):
                    go(act1, acts.at[slot], sa.at[0, j + 1], ra.at[0, j + 1, c], at_x[0][j])
                    go(cot_ref, grads.at[slot], sa.at[2, j + 1], ra.at[1, j + 1, c], at_x[1][j])
                if c == 1:
                    go(act1, acts.at[slot], sa.at[0, 0], ra.at[0, 0, 1], other)
                else:
                    go(cot_ref, grads.at[slot], sa.at[2, 0], ra.at[1, 0, 0], other)

            gather_weights(
                c, own, wg, keep, other, to_z, to_x, to_y, (x, z_hi, y), extra,
                zs, zr, fs, fr, so, ro, s2, r2, s3, r3, sc, rc,
            )

        pl.when(core == c)(run)

    for kernel, target in ((0, wl1), (1, wl2)):
        for j in range(16):
            v = wg[kernel, index_ref[j]].reshape(512, 128)
            base = BLOCK * j
            target[base : base + 180, 0:128] = v[0:180]
            target[base : base + 180, 128:256] = v[192:372]
            target[base : base + 96, 256:320] = v[384:480, 0:64]
            target[base + 96 : base + 180, 256:320] = v[384:468, 64:128]

    def conv(weight):
        result = jnp.zeros((PIX, C), f32)
        for t in range(9):
            ky, kx = t // 3, t % 3
            result = result + jnp.dot(
                pad[kx, 16 * ky : 16 * ky + PIX, :], weight[C * t : C * t + C, :],
                preferred_element_type=f32,
            )
        return result

    second_norm, second_std = group_norm(conv(wl1) + bias_ref[...])
    gate = 1.0 / (1.0 + jnp.exp(-second_norm))
    second_act = (second_norm * gate).astype(bf16)
    act2[...] = second_act

    @pl.when(core == 1)
    def _():
        acts[slot] = act2[...]

    fill(cot_ref[...].astype(f32))
    sent = [
        send(act2, acts.at[slot], sa.at[1, j + 1], ra.at[0, j + 1, core], at_x[1][j]) for j in (1, 0, 2)
    ]

    @pl.when(core == 0)
    def _():
        send(act2, acts.at[slot], sa.at[1, 0], ra.at[0, 0, 0], other)

    act_grad = jnp.zeros((PIX, C), f32)
    for t in range(9):
        ky, kx = 2 - t // 3, 2 - t % 3
        act_grad = act_grad + lax.dot_general(
            pad[kx, 16 * ky : 16 * ky + PIX, :], wl2[C * t : C * t + C, :],
            (((1,), (1,)), ((), ())), preferred_element_type=f32,
        )
    norm_grad = act_grad * gate * (1.0 + second_norm * (1.0 - gate))
    columns = jnp.concatenate(
        [
            jnp.broadcast_to(jnp.sum(norm_grad, axis=0, keepdims=True), (8, C)),
            jnp.broadcast_to(jnp.sum(norm_grad * second_norm, axis=0, keepdims=True), (8, C)),
        ],
        axis=0,
    )
    means = count * jnp.dot(
        columns, member, precision=lax.Precision.HIGHEST, preferred_element_type=f32
    )
    cgrad[...] = (second_std * (norm_grad - means[0:1] - second_norm * means[8:9])).astype(bf16)

    @pl.when(core == 0)
    def _():
        grads[slot] = cgrad[...]

    sent += [
        send(cgrad, grads.at[slot], sa.at[3, j + 1], ra.at[1, j + 1, core], at_x[0][j]) for j in (1, 0, 2)
    ]

    @pl.when(core == 1)
    def _():
        send(cgrad, grads.at[slot], sa.at[3, 0], ra.at[1, 0, 1], other)

    fill(act2[...].astype(f32))
    out_ref[...] = (x_ref[...].astype(f32) + conv(wl2)).astype(bf16)

    def take_acts():
        for d in (1, 2, 3):
            for c in (0, 1):
                pltpu.make_async_copy(acts.at[slot], acts.at[slot], ra.at[0, d, c]).wait()
        pltpu.make_async_copy(acts.at[slot], acts.at[slot], ra.at[0, 0, 1 - core]).wait()

        @pl.loop(0, 8)
        def _(s):
            act_t[:, pl.ds(pl.multiple_of(PIX * s, PIX), PIX)] = acts[s].astype(f32).T.astype(bf16)

    def take_grads():
        for d in (1, 2, 3):
            for c in (0, 1):
                pltpu.make_async_copy(grads.at[slot], grads.at[slot], ra.at[1, d, c]).wait()
        pltpu.make_async_copy(grads.at[slot], grads.at[slot], ra.at[1, 0, 1 - core]).wait()

        @pl.loop(0, 8)
        def _(s):
            v = grads[s].astype(f32)
            for k in range(3):
                pads[k, s, 16:144, :] = shifted(v, k - 1, PIX).astype(bf16)

    @pl.when(core == 0)
    def _():
        take_acts()
        take_grads()
        pltpu.make_async_copy(act2, acts.at[slot], sa.at[1, 0]).wait()

    @pl.when(core == 1)
    def _():
        take_grads()
        take_acts()
        pltpu.make_async_copy(cgrad, grads.at[slot], sa.at[3, 0]).wait()

    for copy in sent:
        copy.wait_send()

    @pl.loop(0, 9)
    def _(t):
        ky, kx = 2 - t // 3, 2 - lax.rem(t, 3)
        rows = pads[kx, :, pl.ds(pl.multiple_of(16 * ky, 16), PIX), :].reshape(8 * PIX, C)
        product = jnp.dot(act_t[...], rows, preferred_element_type=f32)
        total[pl.ds((C // 8) * t, C // 8)] = product.reshape(C // 8, 8, C)

    steps = (2, 1, 3, 0)
    ycopies, lcopies, hcopies = [], [], {}
    for i, step in enumerate(steps):
        holder = lax.rem(z_hi + step, 4)
        ycopies.append([])
        for d in (2, 1, 3, 0):
            column = lax.rem(y + d, 4)
            first = tile_ref[holder * 4 + column]
            v = jnp.concatenate([total[first + n] for n in range(7)], axis=0)
            late = jnp.full((48, C), odd_ref[holder * 4 + column], jnp.int32) > 0
            v = jnp.where(late, v[4:52], v[0:48])
            fold = jnp.concatenate([v[0:24, 256:320], v[24:48, 256:320]], axis=1)
            tile = jnp.concatenate([v[0:48, 0:128], v[0:48, 128:256], fold, jnp.zeros((8, 128), f32)], axis=0)
            part_ref[i, column] = tile.astype(bf16).reshape(NZL, 16, 128)
            if d > 0:
                ycopies[i].append(
                    send(part_ref.at[i, column], ybuf.at[d - 1, i], ys.at[d - 1, i], yr.at[d - 1, i], to_y[d - 1])
                )
    for i in range(4):
        for c in ycopies[i]:
            c.wait()
        v = part_ref[i, y].astype(f32)
        for d in range(3):
            v = v + ybuf[d, i].astype(f32)
        s1[i] = v.astype(bf16)
        lcopies.append([
            send(s1.at[i, lax.rem(z_lo + d, 8)], zbuf.at[d - 1, i], ls.at[d - 1, i], lr.at[d - 1, i], to_l[d - 1])
            for d in (4, 3, 5, 2, 6, 1, 7)
        ])
    for i, step in ((0, 2), (2, 3), (3, 0), (1, 1)):
        for c in lcopies[i]:
            c.wait()
        v = s1[i, z_lo].astype(f32)
        for d in range(7):
            v = v + zbuf[d, i].astype(f32)
        if step == 0:
            own_sum = v
        else:
            if step == 1:
                hcopies[0].wait()
                v = v + hbuf[0].astype(f32)
            s2b[i] = v.astype(bf16)
            hcopies[i] = send(s2b.at[i], hbuf.at[i], hs.at[i], hr.at[i], to_z[3 if step == 3 else 1])
    v = own_sum
    for i in (2, 1):
        hcopies[i].wait()
        v = v + hbuf[i].astype(f32)
    final[...] = (v * (1.0 / SAMPLES)).astype(bf16)

    kept = pltpu.make_async_copy(final, all_ref.at[core, x, z_lo], keep_sem)
    kept.start()
    copies = [
        send(final, all_ref.at[core, x, z_lo], gs.at[d - 1], gr.at[d - 1], to_l[d - 1])
        for d in (4, 3, 5, 2, 6, 1, 7)
    ]
    kept.wait()
    for c in copies:
        c.wait()
    quarter = all_ref.at[core, x]
    copies = [send(quarter, quarter, xs.at[d - 1], xr.at[d - 1], to_x[d - 1]) for d in (2, 1, 3)]
    for c in copies:
        c.wait()
    whole = all_ref.at[core]
    send(whole, whole, cs, cr, other).wait()


def run_step(index, tiles, odd, x, cot, bias, first_weight, second_weight):
    dma = pltpu.SemaphoreType.DMA
    v = pltpu.VMEM
    return pl.pallas_call(
        step_kernel,
        out_shape=(
            jax.ShapeDtypeStruct((PIX, C), bf16),
            jax.ShapeDtypeStruct((2, NX, NZL, 16, 128), bf16),
        ),
        in_specs=[SM, SM, SM, VM, VM, VM, VM, VM],
        out_specs=(VM, VM),
        scratch_shapes=[
            v((2, 4, 2, 64, 128), bf16), v((2, NZH * NY, 4, 2, 64, 128), bf16),
            v((9 * C, C), bf16), v((9 * C, C), bf16), v((3, 160, C), bf16),
            v((PIX, C), bf16), v((PIX, C), bf16), v((PIX, C), bf16),
            v((8, PIX, C), bf16), v((8, PIX, C), bf16), v((C, 8 * PIX), bf16),
            v((3, 8, 160, C), bf16), v((9 * C // 8 + 3, 8, C), f32),
            v((NZH, NY, NZL, 16, 128), bf16), v((3, NZH, NZL, 16, 128), bf16),
            v((NZH, NZL, 16, 128), bf16), v((7, NZH, 16, 128), bf16), v((3, 16, 128), bf16),
            v((3, 16, 128), bf16), v((16, 128), bf16),
            dma((2,)), dma((3, 2)), dma((3, 2)), dma((2,)), dma((2,)), dma((3,)), dma((3,)), dma((3, 3)), dma((3, 3)),
            dma((3, 4, 3)), dma((3, 4, 3)), dma((7,)), dma((7,)), dma((4, 4)), dma((2, 4, 2)),
            dma((3, 4)), dma((3, 4)), dma((7, 4)), dma((7, 4)), dma((3,)), dma((3,)),
            dma((7,)), dma((7,)), dma((3,)), dma((3,)), dma, dma, dma,
        ],
        compiler_params=pltpu.CompilerParams(collective_id=0, has_side_effects=True),
        name="step",
    )(index, tiles, odd, x, cot, bias, first_weight, second_weight)


def finish_kernel(out_ref, all_ref, result_ref, first_ref, second_ref):
    result_ref[...] = out_ref[...]
    for kernel, target in ((0, first_ref), (1, second_ref)):
        for q in range(4):
            v = all_ref[kernel, q].astype(f32).reshape(128, 128)
            base, n = QROWS * q, min(QROWS, BLOCK - QROWS * q)
            target[base : base + n, 0:128] = v[0:n]
            target[base : base + n, 128:256] = v[48 : 48 + n]
            target[base : base + 24, 256:320] = v[96:120, 0:64]
            target[base + 24 : base + n, 256:320] = v[96 : 72 + n, 64:128]


def finish(out, everything):
    grad = jax.ShapeDtypeStruct((BLOCK, C), f32)
    return pl.pallas_call(
        finish_kernel,
        out_shape=(jax.ShapeDtypeStruct((PIX, C), bf16), grad, grad),
        in_specs=[VM, VM],
        out_specs=(VM, VM, VM),
        name="finish",
    )(out, everything)


def time_bias(timestep, time_weight):
    half_dim = TEMB // 2
    frequency = jnp.exp(-math.log(10000.0) * jnp.arange(half_dim, dtype=f32) / half_dim)
    angles = timestep.astype(f32) * frequency
    embedded = jnp.concatenate([jnp.cos(angles), jnp.sin(angles)])
    activated = jax.nn.silu(embedded).astype(bf16)
    return jnp.dot(activated[None, :], time_weight, preferred_element_type=f32)


def body(block_input, cotangent, timesteps, owner_map, time_weight, first_weight, second_weight):
    ids = jnp.arange(16, dtype=jnp.int32)
    inverse = jnp.sum((owner_map[None, :] == ids[:, None]).astype(jnp.int32) * ids[None, :], axis=1)
    quarter = lax.rem(lax.axis_index("rep") // 2, 4)
    starts = inverse * BLOCK + quarter.astype(jnp.int32) * QROWS
    bias = time_bias(timesteps[0], time_weight)
    x = block_input.reshape(PIX, C)
    cot = cotangent.reshape(PIX, C)
    out, everything = run_step(owner_map, starts // 8, lax.rem(starts // 4, 2), x, cot, bias, first_weight, second_weight)
    out, first_grad, second_grad = finish(out, everything)
    return out.reshape(1, HEIGHT, WIDTH, C), first_grad, second_grad


def solution(mesh):
    placed = (
        P(("rep", "dom"), None, None, None),
        P(("rep", "dom"), None, None, None),
        P(("rep", "dom")),
        P(),
        P(),
        P("dom", None),
        P("dom", None),
    )
    return jax.shard_map(
        body,
        mesh=mesh,
        in_specs=placed,
        out_specs=(P(("rep", "dom"), None, None, None), P("dom", None), P("dom", None)),
        check_vma=False,
    )
```

```python
import math

import jax
import jax.numpy as jnp
from jax import lax
from jax.experimental import pallas as pl
from jax.experimental.pallas import tpu as pltpu
from jax.sharding import PartitionSpec as P

C = 320
TEMB = 1280
HEIGHT = 8
WIDTH = 16
PIX = HEIGHT * WIDTH
NX, NY, NZH, NZL = 4, 4, 4, 8
BLOCK = 180
QROWS = 48
SAMPLES = 1024
MESH = pl.DeviceIdType.MESH
norm_eps = 1e-05
bf16 = jnp.bfloat16
f32 = jnp.float32

VM = pl.BlockSpec(memory_space=pltpu.VMEM)
SM = pl.BlockSpec(memory_space=pltpu.SMEM)


def position():
    rep, dom = lax.axis_index("rep"), lax.axis_index("dom")
    return rep // 8, lax.rem(rep // 2, 4), lax.rem(rep, 2), dom // 4, lax.rem(dom, 4)


def device(z_lo, x, core, z_hi, y):
    return {"rep": z_lo * 8 + x * 2 + core, "dom": z_hi * 4 + y}


def send(src, dst, send_sem, recv_sem, target):
    copy = pltpu.make_async_remote_copy(
        src_ref=src, dst_ref=dst, send_sem=send_sem, recv_sem=recv_sem,
        device_id=target, device_id_type=MESH,
    )
    copy.start()
    return copy


def group_matrix():
    row = lax.broadcasted_iota(jnp.int32, (C, C), 0).astype(f32)
    col = lax.broadcasted_iota(jnp.int32, (C, C), 1).astype(f32)
    same = jnp.floor((row + 0.5) * 0.1) == jnp.floor((col + 0.5) * 0.1)
    return jnp.where(same, 1.0, 0.0).astype(f32)


def shifted(v, step, rows):
    if step == 0:
        return v
    column = lax.rem(lax.broadcasted_iota(jnp.int32, (rows, C), 0), WIDTH)
    inside = (column + step >= 0) & (column + step < WIDTH)
    return jnp.where(inside, pltpu.roll(v, (-step) % rows, 0), 0.0)


def pack_map(v):
    fold = jnp.concatenate([v[0:64, 256:320], v[64:128, 256:320]], axis=1)
    return jnp.concatenate([v[:, 0:128], v[:, 128:256], fold], axis=0).astype(bf16)


def unpack_map(p):
    p = p.astype(f32)
    tail = jnp.concatenate([p[256:320, 0:64], p[256:320, 64:128]], axis=0)
    return jnp.concatenate([p[0:128], p[128:256], tail], axis=1)


def pack_block(w):
    w = w.astype(f32)
    pad = jnp.zeros((12, 128), f32)
    fold = jnp.concatenate(
        [w[0:96, 256:320], jnp.concatenate([w[96:180, 256:320], jnp.zeros((12, 64), f32)], axis=0)], axis=1
    )
    tiles = jnp.concatenate([w[:, 0:128], pad, w[:, 128:256], pad, fold, jnp.zeros((32, 128), f32)], axis=0)
    return tiles.astype(bf16).reshape(4, 2, 64, 128)


def gather_weights(c, own, wg, keep, other, to_z, to_x, to_y, place, extra, zs, zr, fs, fr, so, ro, s2, r2, s3, r3, sc, rc):
    x, z_hi, y = place
    sent = []

    def go(*copy):
        sent.append(send(*copy))
        return sent[-1]

    def arrived(copies):
        for copy in copies:
            copy.wait_recv()

    def block(d):
        return lax.rem(z_hi + 4 - d, 4)

    zc = {
        (d, h): go(own.at[c, x, h], wg.at[c, z_hi * 4 + y, x, h], zs.at[d - 1, h], zr.at[d - 1, h], to_z[d])
        for d, h in ((1, 1), (3, 0), (1, 0), (3, 1))
    }
    oc = [go(own.at[c], wg.at[c, z_hi * 4 + y], so.at[j], ro.at[j], to_y[j]) for j in (1, 0, 2)]
    extra(go)
    near, far = (to_x, to_y) if c == 0 else (to_y, to_x)

    def relay(d, h):
        arrived([zc[d, h]])
        part = wg.at[c, block(d) * 4 + y, x, h]
        return go(part, part, fs.at[h], fr.at[h], to_z[d])

    def second(d, before):
        arrived(before)
        part = wg.at[c, block(d) * 4 + y, x]
        return [go(part, part, s2.at[d - 1, j], r2.at[d - 1, j], near[j]) for j in (1, 0, 2)]

    def third(d, before):
        arrived(before)
        if c == 0:
            part = wg.at[0, block(d) * 4 + y]
            return {j + 1: go(part, part, s3.at[d - 1, 0, j], r3.at[d - 1, 0, j], far[j]) for j in (1, 0, 2)}
        copies = {}
        for i in range(4):
            part = wg.at[1, block(d) * 4 + lax.rem(y + i, 4), x]
            for j in (1, 0, 2):
                copies[i, j] = go(part, part, s3.at[d - 1, i, j], r3.at[d - 1, i, j], far[j])
        return copies

    def fourth(d, before):
        copies = []
        for i in range(4):
            if c == 0:
                arrived([before[4 - i]] if i > 0 else [])
            else:
                arrived([before[i, j] for j in range(3)])
            part = wg.at[c, block(d) * 4 + lax.rem(y + i, 4)]
            copies.append(go(part, part, sc.at[d, i], rc.at[d, i], other))
        return copies

    for copy in keep:
        copy.wait()
    upper = relay(1, 1)
    lower = relay(3, 0)
    a1 = second(1, [zc[1, 0]])
    a3 = second(3, [zc[3, 1]])
    b1 = third(1, a1)
    b3 = third(3, a3)
    arrived(oc)
    last = []
    for i in (1, 2, 3):
        part = wg.at[c, z_hi * 4 + lax.rem(y + i, 4)]
        last.append(go(part, part, sc.at[0, i], rc.at[0, i], other))
    a2 = second(2, [upper, lower])
    last += fourth(1, b1)
    b2 = third(2, a2)
    last += fourth(3, b3)
    last += fourth(2, b2)
    arrived(last)
    for copy in sent:
        copy.wait_send()


def step_kernel(
    index_ref, tile_ref, odd_ref, x_ref, cot_ref, bias_ref, w1_ref, w2_ref,
    out_ref, all_ref,
    own, wg, wl1, wl2, pad, act1, act2, cgrad, cots, acts, grads, act_t, pads, total,
    part_ref, ybuf, s1, zbuf, s2b, hbuf, final,
    own_sem, zs, zr, fs, fr, so, ro, s2, r2, s3, r3, sc, rc, sa, ra,
    ys, yr, ls, lr, hs, hr, gs, gr, xs, xr, cs, cr, keep_sem,
):
    z_lo, x, core, z_hi, y = position()
    slot = x * 2 + core
    to_z = {d: device(z_lo, x, core, lax.rem(z_hi + d, 4), y) for d in (1, 3)}
    to_y = [device(z_lo, x, core, z_hi, lax.rem(y + d, 4)) for d in (1, 2, 3)]
    to_l = [device(lax.rem(z_lo + d, 8), x, core, z_hi, y) for d in range(1, 8)]
    at_x = [[device(z_lo, lax.rem(x + d, 4), c, z_hi, y) for d in (1, 2, 3)] for c in (0, 1)]
    to_x = [device(z_lo, lax.rem(x + d, 4), core, z_hi, y) for d in (1, 2, 3)]
    other = device(z_lo, x, 1 - core, z_hi, y)
    partners = [to_z[1], to_z[3]] + to_y + to_l + at_x[0] + at_x[1] + [other]
    barrier = pltpu.get_barrier_semaphore()
    for partner in partners:
        pl.semaphore_signal(barrier, inc=1, device_id=partner, device_id_type=MESH)

    member = group_matrix()
    count = 1.0 / (PIX * 10)

    def group_mean(v):
        column = jnp.sum(v, axis=0, keepdims=True)
        return jnp.dot(
            jnp.broadcast_to(column, (8, C)), member,
            precision=lax.Precision.HIGHEST, preferred_element_type=f32,
        )[0:1] * count

    def group_norm(v):
        centered = v - group_mean(v)
        inverse_std = lax.rsqrt(group_mean(centered * centered) + norm_eps)
        return centered * inverse_std, inverse_std

    own[0] = pack_block(w1_ref[...])
    own[1] = pack_block(w2_ref[...])
    source = x_ref[...].astype(f32)
    normed, _ = group_norm(source)
    first_act = (normed * (1.0 / (1.0 + jnp.exp(-normed)))).astype(bf16).astype(f32)
    act1[...] = pack_map(first_act)
    cots[...] = pack_map(cot_ref[...].astype(f32))
    pad[:, 0:16, :] = jnp.zeros((3, 16, C), bf16)
    pad[:, 144:160, :] = jnp.zeros((3, 16, C), bf16)
    pads[:, :, 0:16, :] = jnp.zeros((3, 8, 16, C), bf16)
    pads[:, :, 144:160, :] = jnp.zeros((3, 8, 16, C), bf16)
    total[9 * C // 8 :] = jnp.zeros((3, 8, C), f32)

    def fill(v):
        for k in range(3):
            pad[k, 16:144, :] = shifted(v, k - 1, PIX).astype(bf16)

    fill(first_act)

    @pl.when(core == 0)
    def _():
        acts[slot] = act1[...]

    @pl.when(core == 1)
    def _():
        grads[slot] = cots[...]

    pl.semaphore_wait(barrier, len(partners))

    keep = [pltpu.make_async_copy(own.at[k], wg.at[k, z_hi * 4 + y], own_sem.at[k]) for k in (0, 1)]
    for copy in keep:
        copy.start()

    for c in (0, 1):

        def run(c=c):
            def extra(go):
                for j in (1, 0, 2):
                    go(act1, acts.at[slot], sa.at[0, j + 1], ra.at[0, j + 1, c], at_x[0][j])
                    go(cots, grads.at[slot], sa.at[2, j + 1], ra.at[1, j + 1, c], at_x[1][j])
                if c == 1:
                    go(act1, acts.at[slot], sa.at[0, 0], ra.at[0, 0, 1], other)
                else:
                    go(cots, grads.at[slot], sa.at[2, 0], ra.at[1, 0, 0], other)

            gather_weights(
                c, own, wg, keep, other, to_z, to_x, to_y, (x, z_hi, y), extra,
                zs, zr, fs, fr, so, ro, s2, r2, s3, r3, sc, rc,
            )

        pl.when(core == c)(run)

    for kernel, target in ((0, wl1), (1, wl2)):
        for j in range(16):
            v = wg[kernel, index_ref[j]].reshape(512, 128)
            base = BLOCK * j
            target[base : base + 180, 0:128] = v[0:180]
            target[base : base + 180, 128:256] = v[192:372]
            target[base : base + 96, 256:320] = v[384:480, 0:64]
            target[base + 96 : base + 180, 256:320] = v[384:468, 64:128]

    def conv(weight):
        result = jnp.zeros((PIX, C), f32)
        for t in range(9):
            ky, kx = t // 3, t % 3
            result = result + jnp.dot(
                pad[kx, 16 * ky : 16 * ky + PIX, :], weight[C * t : C * t + C, :],
                preferred_element_type=f32,
            )
        return result

    second_norm, second_std = group_norm(conv(wl1) + bias_ref[...])
    gate = 1.0 / (1.0 + jnp.exp(-second_norm))
    second_act = (second_norm * gate).astype(bf16).astype(f32)
    act2[...] = pack_map(second_act)

    @pl.when(core == 1)
    def _():
        acts[slot] = act2[...]

    fill(cot_ref[...].astype(f32))
    sent = [
        send(act2, acts.at[slot], sa.at[1, j + 1], ra.at[0, j + 1, core], at_x[1][j]) for j in (1, 0, 2)
    ]

    @pl.when(core == 0)
    def _():
        send(act2, acts.at[slot], sa.at[1, 0], ra.at[0, 0, 0], other)

    act_grad = jnp.zeros((PIX, C), f32)
    for t in range(9):
        ky, kx = 2 - t // 3, 2 - t % 3
        act_grad = act_grad + lax.dot_general(
            pad[kx, 16 * ky : 16 * ky + PIX, :], wl2[C * t : C * t + C, :],
            (((1,), (1,)), ((), ())), preferred_element_type=f32,
        )
    norm_grad = act_grad * gate * (1.0 + second_norm * (1.0 - gate))
    columns = jnp.concatenate(
        [
            jnp.broadcast_to(jnp.sum(norm_grad, axis=0, keepdims=True), (8, C)),
            jnp.broadcast_to(jnp.sum(norm_grad * second_norm, axis=0, keepdims=True), (8, C)),
        ],
        axis=0,
    )
    means = count * jnp.dot(
        columns, member, precision=lax.Precision.HIGHEST, preferred_element_type=f32
    )
    cgrad[...] = pack_map(second_std * (norm_grad - means[0:1] - second_norm * means[8:9]))

    @pl.when(core == 0)
    def _():
        grads[slot] = cgrad[...]

    sent += [
        send(cgrad, grads.at[slot], sa.at[3, j + 1], ra.at[1, j + 1, core], at_x[0][j]) for j in (1, 0, 2)
    ]

    @pl.when(core == 1)
    def _():
        send(cgrad, grads.at[slot], sa.at[3, 0], ra.at[1, 0, 1], other)

    fill(unpack_map(act2[...]))
    out_ref[...] = (x_ref[...].astype(f32) + conv(wl2)).astype(bf16)

    def take_acts():
        for d in (1, 2, 3):
            for c in (0, 1):
                pltpu.make_async_copy(acts.at[slot], acts.at[slot], ra.at[0, d, c]).wait()
        pltpu.make_async_copy(acts.at[slot], acts.at[slot], ra.at[0, 0, 1 - core]).wait()

        @pl.loop(0, 8)
        def _(s):
            act_t[:, pl.ds(pl.multiple_of(PIX * s, PIX), PIX)] = unpack_map(acts[s]).T.astype(bf16)

    def take_grads():
        for d in (1, 2, 3):
            for c in (0, 1):
                pltpu.make_async_copy(grads.at[slot], grads.at[slot], ra.at[1, d, c]).wait()
        pltpu.make_async_copy(grads.at[slot], grads.at[slot], ra.at[1, 0, 1 - core]).wait()

        @pl.loop(0, 8)
        def _(s):
            v = unpack_map(grads[s])
            for k in range(3):
                pads[k, s, 16:144, :] = shifted(v, k - 1, PIX).astype(bf16)

    @pl.when(core == 0)
    def _():
        take_acts()
        take_grads()
        pltpu.make_async_copy(act2, acts.at[slot], sa.at[1, 0]).wait()

    @pl.when(core == 1)
    def _():
        take_grads()
        take_acts()
        pltpu.make_async_copy(cgrad, grads.at[slot], sa.at[3, 0]).wait()

    for copy in sent:
        copy.wait_send()

    @pl.loop(0, 9)
    def _(t):
        ky, kx = 2 - t // 3, 2 - lax.rem(t, 3)
        rows = pads[kx, :, pl.ds(pl.multiple_of(16 * ky, 16), PIX), :].reshape(8 * PIX, C)
        product = jnp.dot(act_t[...], rows, preferred_element_type=f32)
        total[pl.ds((C // 8) * t, C // 8)] = product.reshape(C // 8, 8, C)

    steps = (2, 1, 3, 0)
    ycopies, lcopies, hcopies = [], [], {}
    for i, step in enumerate(steps):
        holder = lax.rem(z_hi + step, 4)
        ycopies.append([])
        for d in (2, 1, 3, 0):
            column = lax.rem(y + d, 4)
            first = tile_ref[holder * 4 + column]
            v = jnp.concatenate([total[first + n] for n in range(7)], axis=0)
            late = jnp.full((48, C), odd_ref[holder * 4 + column], jnp.int32) > 0
            v = jnp.where(late, v[4:52], v[0:48])
            fold = jnp.concatenate([v[0:24, 256:320], v[24:48, 256:320]], axis=1)
            tile = jnp.concatenate([v[0:48, 0:128], v[0:48, 128:256], fold, jnp.zeros((8, 128), f32)], axis=0)
            part_ref[i, column] = tile.astype(bf16).reshape(NZL, 16, 128)
            if d > 0:
                ycopies[i].append(
                    send(part_ref.at[i, column], ybuf.at[d - 1, i], ys.at[d - 1, i], yr.at[d - 1, i], to_y[d - 1])
                )
    for i in range(4):
        for c in ycopies[i]:
            c.wait()
        v = part_ref[i, y].astype(f32)
        for d in range(3):
            v = v + ybuf[d, i].astype(f32)
        s1[i] = v.astype(bf16)
        lcopies.append([
            send(s1.at[i, lax.rem(z_lo + d, 8)], zbuf.at[d - 1, i], ls.at[d - 1, i], lr.at[d - 1, i], to_l[d - 1])
            for d in (4, 3, 5, 2, 6, 1, 7)
        ])
    for i, step in ((0, 2), (2, 3), (3, 0), (1, 1)):
        for c in lcopies[i]:
            c.wait()
        v = s1[i, z_lo].astype(f32)
        for d in range(7):
            v = v + zbuf[d, i].astype(f32)
        if step == 0:
            own_sum = v
        else:
            if step == 1:
                hcopies[0].wait()
                v = v + hbuf[0].astype(f32)
            s2b[i] = v.astype(bf16)
            hcopies[i] = send(s2b.at[i], hbuf.at[i], hs.at[i], hr.at[i], to_z[3 if step == 3 else 1])
    v = own_sum
    for i in (2, 1):
        hcopies[i].wait()
        v = v + hbuf[i].astype(f32)
    final[...] = (v * (1.0 / SAMPLES)).astype(bf16)

    kept = pltpu.make_async_copy(final, all_ref.at[core, x, z_lo], keep_sem)
    kept.start()
    copies = [
        send(final, all_ref.at[core, x, z_lo], gs.at[d - 1], gr.at[d - 1], to_l[d - 1])
        for d in (4, 3, 5, 2, 6, 1, 7)
    ]
    kept.wait()
    for c in copies:
        c.wait()
    quarter = all_ref.at[core, x]
    copies = [send(quarter, quarter, xs.at[d - 1], xr.at[d - 1], to_x[d - 1]) for d in (2, 1, 3)]
    for c in copies:
        c.wait()
    whole = all_ref.at[core]
    send(whole, whole, cs, cr, other).wait()


def run_step(index, tiles, odd, x, cot, bias, first_weight, second_weight):
    dma = pltpu.SemaphoreType.DMA
    v = pltpu.VMEM
    return pl.pallas_call(
        step_kernel,
        out_shape=(
            jax.ShapeDtypeStruct((PIX, C), bf16),
            jax.ShapeDtypeStruct((2, NX, NZL, 16, 128), bf16),
        ),
        in_specs=[SM, SM, SM, VM, VM, VM, VM, VM],
        out_specs=(VM, VM),
        scratch_shapes=[
            v((2, 4, 2, 64, 128), bf16), v((2, NZH * NY, 4, 2, 64, 128), bf16),
            v((9 * C, C), bf16), v((9 * C, C), bf16), v((3, 160, C), bf16),
            v((C, 128), bf16), v((C, 128), bf16), v((C, 128), bf16), v((C, 128), bf16),
            v((8, C, 128), bf16), v((8, C, 128), bf16), v((C, 8 * PIX), bf16),
            v((3, 8, 160, C), bf16), v((9 * C // 8 + 3, 8, C), f32),
            v((NZH, NY, NZL, 16, 128), bf16), v((3, NZH, NZL, 16, 128), bf16),
            v((NZH, NZL, 16, 128), bf16), v((7, NZH, 16, 128), bf16), v((3, 16, 128), bf16),
            v((3, 16, 128), bf16), v((16, 128), bf16),
            dma((2,)), dma((3, 2)), dma((3, 2)), dma((2,)), dma((2,)), dma((3,)), dma((3,)), dma((3, 3)), dma((3, 3)),
            dma((3, 4, 3)), dma((3, 4, 3)), dma((4, 4)), dma((4, 4)), dma((4, 4)), dma((2, 4, 2)),
            dma((3, 4)), dma((3, 4)), dma((7, 4)), dma((7, 4)), dma((3,)), dma((3,)),
            dma((7,)), dma((7,)), dma((3,)), dma((3,)), dma, dma, dma,
        ],
        compiler_params=pltpu.CompilerParams(collective_id=0, has_side_effects=True),
        name="step",
    )(index, tiles, odd, x, cot, bias, first_weight, second_weight)


def finish_kernel(out_ref, all_ref, result_ref, first_ref, second_ref):
    result_ref[...] = out_ref[...]
    for kernel, target in ((0, first_ref), (1, second_ref)):
        for q in range(4):
            v = all_ref[kernel, q].astype(f32).reshape(128, 128)
            base, n = QROWS * q, min(QROWS, BLOCK - QROWS * q)
            target[base : base + n, 0:128] = v[0:n]
            target[base : base + n, 128:256] = v[48 : 48 + n]
            target[base : base + 24, 256:320] = v[96:120, 0:64]
            target[base + 24 : base + n, 256:320] = v[96 : 72 + n, 64:128]


def finish(out, everything):
    grad = jax.ShapeDtypeStruct((BLOCK, C), f32)
    return pl.pallas_call(
        finish_kernel,
        out_shape=(jax.ShapeDtypeStruct((PIX, C), bf16), grad, grad),
        in_specs=[VM, VM],
        out_specs=(VM, VM, VM),
        name="finish",
    )(out, everything)


def time_bias(timestep, time_weight):
    half_dim = TEMB // 2
    frequency = jnp.exp(-math.log(10000.0) * jnp.arange(half_dim, dtype=f32) / half_dim)
    angles = timestep.astype(f32) * frequency
    embedded = jnp.concatenate([jnp.cos(angles), jnp.sin(angles)])
    activated = jax.nn.silu(embedded).astype(bf16)
    return jnp.dot(activated[None, :], time_weight, preferred_element_type=f32)


def body(block_input, cotangent, timesteps, owner_map, time_weight, first_weight, second_weight):
    ids = jnp.arange(16, dtype=jnp.int32)
    inverse = jnp.sum((owner_map[None, :] == ids[:, None]).astype(jnp.int32) * ids[None, :], axis=1)
    quarter = lax.rem(lax.axis_index("rep") // 2, 4)
    starts = inverse * BLOCK + quarter.astype(jnp.int32) * QROWS
    bias = time_bias(timesteps[0], time_weight)
    x = block_input.reshape(PIX, C)
    cot = cotangent.reshape(PIX, C)
    out, everything = run_step(owner_map, starts // 8, lax.rem(starts // 4, 2), x, cot, bias, first_weight, second_weight)
    out, first_grad, second_grad = finish(out, everything)
    return out.reshape(1, HEIGHT, WIDTH, C), first_grad, second_grad


def solution(mesh):
    placed = (
        P(("rep", "dom"), None, None, None),
        P(("rep", "dom"), None, None, None),
        P(("rep", "dom")),
        P(),
        P(),
        P("dom", None),
        P("dom", None),
    )
    return jax.shard_map(
        body,
        mesh=mesh,
        in_specs=placed,
        out_specs=(P(("rep", "dom"), None, None, None), P("dom", None), P("dom", None)),
        check_vma=False,
    )
```

```python
import math

import jax
import jax.numpy as jnp
from jax import lax
from jax.experimental import pallas as pl
from jax.experimental.pallas import tpu as pltpu
from jax.sharding import PartitionSpec as P

C = 320
TEMB = 1280
HEIGHT = 8
WIDTH = 16
PIX = HEIGHT * WIDTH
NX, NY, NZH, NZL = 4, 4, 4, 8
BLOCK = 180
QROWS = 48
SAMPLES = 1024
MESH = pl.DeviceIdType.MESH
norm_eps = 1e-05
bf16 = jnp.bfloat16
f32 = jnp.float32

VM = pl.BlockSpec(memory_space=pltpu.VMEM)
SM = pl.BlockSpec(memory_space=pltpu.SMEM)


def position():
    rep, dom = lax.axis_index("rep"), lax.axis_index("dom")
    return rep // 8, lax.rem(rep // 2, 4), lax.rem(rep, 2), dom // 4, lax.rem(dom, 4)


def device(z_lo, x, core, z_hi, y):
    return {"rep": z_lo * 8 + x * 2 + core, "dom": z_hi * 4 + y}


def send(src, dst, send_sem, recv_sem, target):
    copy = pltpu.make_async_remote_copy(
        src_ref=src, dst_ref=dst, send_sem=send_sem, recv_sem=recv_sem,
        device_id=target, device_id_type=MESH,
    )
    copy.start()
    return copy


def group_matrix():
    row = lax.broadcasted_iota(jnp.int32, (C, C), 0).astype(f32)
    col = lax.broadcasted_iota(jnp.int32, (C, C), 1).astype(f32)
    same = jnp.floor((row + 0.5) * 0.1) == jnp.floor((col + 0.5) * 0.1)
    return jnp.where(same, 1.0, 0.0).astype(f32)


def shifted(v, step, rows):
    if step == 0:
        return v
    column = lax.rem(lax.broadcasted_iota(jnp.int32, (rows, C), 0), WIDTH)
    inside = (column + step >= 0) & (column + step < WIDTH)
    return jnp.where(inside, pltpu.roll(v, (-step) % rows, 0), 0.0)


def pack_map(v):
    fold = jnp.concatenate([v[0:64, 256:320], v[64:128, 256:320]], axis=1)
    return jnp.concatenate([v[:, 0:128], v[:, 128:256], fold], axis=0).astype(bf16)


def unpack_map(p):
    p = p.astype(f32)
    tail = jnp.concatenate([p[256:320, 0:64], p[256:320, 64:128]], axis=0)
    return jnp.concatenate([p[0:128], p[128:256], tail], axis=1)


def pack_block(w):
    w = w.astype(f32)
    pad = jnp.zeros((12, 128), f32)
    fold = jnp.concatenate(
        [w[0:96, 256:320], jnp.concatenate([w[96:180, 256:320], jnp.zeros((12, 64), f32)], axis=0)], axis=1
    )
    tiles = jnp.concatenate([w[:, 0:128], pad, w[:, 128:256], pad, fold, jnp.zeros((32, 128), f32)], axis=0)
    return tiles.astype(bf16).reshape(4, 2, 64, 128)


def gather_weights(c, own, wg, keep, other, to_z, to_x, to_y, place, extra, zs, zr, fs, fr, so, ro, s2, r2, s3, r3, sc, rc):
    x, z_hi, y = place
    sent = []

    def go(*copy):
        sent.append(send(*copy))
        return sent[-1]

    def arrived(copies):
        for copy in copies:
            copy.wait_recv()

    def block(d):
        return lax.rem(z_hi + 4 - d, 4)

    zc = {
        (d, h): go(own.at[c, x, h], wg.at[c, z_hi * 4 + y, x, h], zs.at[d - 1, h], zr.at[d - 1, h], to_z[d])
        for d, h in ((1, 1), (3, 0), (1, 0), (3, 1))
    }
    oc = [go(own.at[c], wg.at[c, z_hi * 4 + y], so.at[j], ro.at[j], to_y[j]) for j in (1, 0, 2)]
    extra(go)
    near, far = (to_x, to_y) if c == 0 else (to_y, to_x)

    def relay(d, h):
        arrived([zc[d, h]])
        part = wg.at[c, block(d) * 4 + y, x, h]
        return go(part, part, fs.at[h], fr.at[h], to_z[d])

    def second(d, before):
        arrived(before)
        part = wg.at[c, block(d) * 4 + y, x]
        return [go(part, part, s2.at[d - 1, j], r2.at[d - 1, j], near[j]) for j in (1, 0, 2)]

    def third(d, before):
        arrived(before)
        if c == 0:
            part = wg.at[0, block(d) * 4 + y]
            return {j + 1: go(part, part, s3.at[d - 1, 0, j], r3.at[d - 1, 0, j], far[j]) for j in (1, 0, 2)}
        copies = {}
        for i in range(4):
            part = wg.at[1, block(d) * 4 + lax.rem(y + i, 4), x]
            for j in (1, 0, 2):
                copies[i, j] = go(part, part, s3.at[d - 1, i, j], r3.at[d - 1, i, j], far[j])
        return copies

    def fourth(d, before):
        copies = []
        for i in range(4):
            if c == 0:
                arrived([before[4 - i]] if i > 0 else [])
            else:
                arrived([before[i, j] for j in range(3)])
            part = wg.at[c, block(d) * 4 + lax.rem(y + i, 4)]
            copies.append(go(part, part, sc.at[d, i], rc.at[d, i], other))
        return copies

    for copy in keep:
        copy.wait()
    upper = relay(1, 1)
    lower = relay(3, 0)
    a1 = second(1, [zc[1, 0]])
    a3 = second(3, [zc[3, 1]])
    b1 = third(1, a1)
    b3 = third(3, a3)
    arrived(oc)
    last = []
    for i in (1, 2, 3):
        part = wg.at[c, z_hi * 4 + lax.rem(y + i, 4)]
        last.append(go(part, part, sc.at[0, i], rc.at[0, i], other))
    a2 = second(2, [upper, lower])
    last += fourth(1, b1)
    b2 = third(2, a2)
    last += fourth(3, b3)
    last += fourth(2, b2)
    arrived(last)
    for copy in sent:
        copy.wait_send()


def step_kernel(
    index_ref, tile_ref, odd_ref, x_ref, cot_ref, bias_ref, w1_ref, w2_ref,
    out_ref, all_ref,
    own, wg, wl1, wl2, pad, act1, act2, cgrad, cots, acts, grads, act_t, pads, total,
    part_ref, ybuf, s1, zbuf, s2b, hbuf, final,
    own_sem, zs, zr, fs, fr, so, ro, s2, r2, s3, r3, sc, rc, sa, ra,
    ys, yr, ls, lr, hs, hr, gs, gr, xs, xr, cs, cr, keep_sem,
):
    z_lo, x, core, z_hi, y = position()
    slot = x * 2 + core
    to_z = {d: device(z_lo, x, core, lax.rem(z_hi + d, 4), y) for d in (1, 3)}
    to_y = [device(z_lo, x, core, z_hi, lax.rem(y + d, 4)) for d in (1, 2, 3)]
    to_l = [device(lax.rem(z_lo + d, 8), x, core, z_hi, y) for d in range(1, 8)]
    at_x = [[device(z_lo, lax.rem(x + d, 4), c, z_hi, y) for d in (1, 2, 3)] for c in (0, 1)]
    to_x = [device(z_lo, lax.rem(x + d, 4), core, z_hi, y) for d in (1, 2, 3)]
    other = device(z_lo, x, 1 - core, z_hi, y)
    partners = [to_z[1], to_z[3]] + to_y + to_l + at_x[0] + at_x[1] + [other]
    barrier = pltpu.get_barrier_semaphore()
    for partner in partners:
        pl.semaphore_signal(barrier, inc=1, device_id=partner, device_id_type=MESH)

    member = group_matrix()
    count = 1.0 / (PIX * 10)

    def group_mean(v):
        column = jnp.sum(v, axis=0, keepdims=True)
        return jnp.dot(
            jnp.broadcast_to(column, (8, C)), member,
            precision=lax.Precision.HIGHEST, preferred_element_type=f32,
        )[0:1] * count

    def group_norm(v):
        centered = v - group_mean(v)
        inverse_std = lax.rsqrt(group_mean(centered * centered) + norm_eps)
        return centered * inverse_std, inverse_std

    own[0] = pack_block(w1_ref[...])
    own[1] = pack_block(w2_ref[...])
    source = x_ref[...].astype(f32)
    normed, _ = group_norm(source)
    first_act = (normed * (1.0 / (1.0 + jnp.exp(-normed)))).astype(bf16).astype(f32)
    act1[...] = pack_map(first_act)
    cots[...] = pack_map(cot_ref[...].astype(f32))
    pad[:, 0:16, :] = jnp.zeros((3, 16, C), bf16)
    pad[:, 144:160, :] = jnp.zeros((3, 16, C), bf16)
    pads[:, :, 0:16, :] = jnp.zeros((3, 8, 16, C), bf16)
    pads[:, :, 144:160, :] = jnp.zeros((3, 8, 16, C), bf16)
    total[9 * C // 8 :] = jnp.zeros((3, 8, C), f32)

    def fill(v):
        for k in range(3):
            pad[k, 16:144, :] = shifted(v, k - 1, PIX).astype(bf16)

    fill(first_act)

    @pl.when(core == 0)
    def _():
        acts[slot] = act1[...]

    @pl.when(core == 1)
    def _():
        grads[slot] = cots[...]

    pl.semaphore_wait(barrier, len(partners))

    keep = [pltpu.make_async_copy(own.at[k], wg.at[k, z_hi * 4 + y], own_sem.at[k]) for k in (0, 1)]
    for copy in keep:
        copy.start()

    for c in (0, 1):

        def run(c=c):
            def extra(go):
                for j in (1, 0, 2):
                    go(act1, acts.at[slot], sa.at[0, j + 1], ra.at[0, j + 1, c], at_x[0][j])
                    go(cots, grads.at[slot], sa.at[2, j + 1], ra.at[1, j + 1, c], at_x[1][j])
                if c == 1:
                    go(act1, acts.at[slot], sa.at[0, 0], ra.at[0, 0, 1], other)
                else:
                    go(cots, grads.at[slot], sa.at[2, 0], ra.at[1, 0, 0], other)

            gather_weights(
                c, own, wg, keep, other, to_z, to_x, to_y, (x, z_hi, y), extra,
                zs, zr, fs, fr, so, ro, s2, r2, s3, r3, sc, rc,
            )

        pl.when(core == c)(run)

    for kernel, target in ((0, wl1), (1, wl2)):
        for j in range(16):
            v = wg[kernel, index_ref[j]].reshape(512, 128)
            base = BLOCK * j
            target[base : base + 180, 0:128] = v[0:180]
            target[base : base + 180, 128:256] = v[192:372]
            target[base : base + 96, 256:320] = v[384:480, 0:64]
            target[base + 96 : base + 180, 256:320] = v[384:468, 64:128]

    def conv(weight):
        result = jnp.zeros((PIX, C), f32)
        for t in range(9):
            ky, kx = t // 3, t % 3
            result = result + jnp.dot(
                pad[kx, 16 * ky : 16 * ky + PIX, :], weight[C * t : C * t + C, :],
                preferred_element_type=f32,
            )
        return result

    second_norm, second_std = group_norm(conv(wl1) + bias_ref[...])
    gate = 1.0 / (1.0 + jnp.exp(-second_norm))
    second_act = (second_norm * gate).astype(bf16).astype(f32)
    act2[...] = pack_map(second_act)

    @pl.when(core == 1)
    def _():
        acts[slot] = act2[...]

    fill(cot_ref[...].astype(f32))
    sent = [
        send(act2, acts.at[slot], sa.at[1, j + 1], ra.at[0, j + 1, core], at_x[1][j]) for j in (1, 0, 2)
    ]

    @pl.when(core == 0)
    def _():
        send(act2, acts.at[slot], sa.at[1, 0], ra.at[0, 0, 0], other)

    act_grad = jnp.zeros((PIX, C), f32)
    for t in range(9):
        ky, kx = 2 - t // 3, 2 - t % 3
        act_grad = act_grad + lax.dot_general(
            pad[kx, 16 * ky : 16 * ky + PIX, :], wl2[C * t : C * t + C, :],
            (((1,), (1,)), ((), ())), preferred_element_type=f32,
        )
    norm_grad = act_grad * gate * (1.0 + second_norm * (1.0 - gate))
    columns = jnp.concatenate(
        [
            jnp.broadcast_to(jnp.sum(norm_grad, axis=0, keepdims=True), (8, C)),
            jnp.broadcast_to(jnp.sum(norm_grad * second_norm, axis=0, keepdims=True), (8, C)),
        ],
        axis=0,
    )
    means = count * jnp.dot(
        columns, member, precision=lax.Precision.HIGHEST, preferred_element_type=f32
    )
    cgrad[...] = pack_map(second_std * (norm_grad - means[0:1] - second_norm * means[8:9]))

    @pl.when(core == 0)
    def _():
        grads[slot] = cgrad[...]

    sent += [
        send(cgrad, grads.at[slot], sa.at[3, j + 1], ra.at[1, j + 1, core], at_x[0][j]) for j in (1, 0, 2)
    ]

    @pl.when(core == 1)
    def _():
        send(cgrad, grads.at[slot], sa.at[3, 0], ra.at[1, 0, 1], other)

    fill(unpack_map(act2[...]))
    out_ref[...] = (x_ref[...].astype(f32) + conv(wl2)).astype(bf16)

    def take_acts():
        for d in (1, 2, 3):
            for c in (0, 1):
                pltpu.make_async_copy(acts.at[slot], acts.at[slot], ra.at[0, d, c]).wait()
        pltpu.make_async_copy(acts.at[slot], acts.at[slot], ra.at[0, 0, 1 - core]).wait()

        @pl.loop(0, 8)
        def _(s):
            act_t[:, pl.ds(pl.multiple_of(PIX * s, PIX), PIX)] = unpack_map(acts[s]).T.astype(bf16)

    def take_grads():
        for d in (1, 2, 3):
            for c in (0, 1):
                pltpu.make_async_copy(grads.at[slot], grads.at[slot], ra.at[1, d, c]).wait()
        pltpu.make_async_copy(grads.at[slot], grads.at[slot], ra.at[1, 0, 1 - core]).wait()

        @pl.loop(0, 8)
        def _(s):
            v = unpack_map(grads[s])
            for k in range(3):
                pads[k, s, 16:144, :] = shifted(v, k - 1, PIX).astype(bf16)

    @pl.when(core == 0)
    def _():
        take_acts()
        take_grads()
        pltpu.make_async_copy(act2, acts.at[slot], sa.at[1, 0]).wait()

    @pl.when(core == 1)
    def _():
        take_grads()
        take_acts()
        pltpu.make_async_copy(cgrad, grads.at[slot], sa.at[3, 0]).wait()

    for copy in sent:
        copy.wait_send()

    @pl.loop(0, 9)
    def _(t):
        ky, kx = 2 - t // 3, 2 - lax.rem(t, 3)
        rows = pads[kx, :, pl.ds(pl.multiple_of(16 * ky, 16), PIX), :].reshape(8 * PIX, C)
        product = jnp.dot(act_t[...], rows, preferred_element_type=f32)
        total[pl.ds((C // 8) * t, C // 8)] = product.reshape(C // 8, 8, C)

    steps = (2, 1, 3, 0)
    ycopies, lcopies, hcopies = [], [], {}
    for i, step in enumerate(steps):
        holder = lax.rem(z_hi + step, 4)
        ycopies.append([])
        for d in (2, 1, 3, 0):
            column = lax.rem(y + d, 4)
            first = tile_ref[holder * 4 + column]
            v = jnp.concatenate([total[first + n] for n in range(7)], axis=0)
            late = jnp.full((48, C), odd_ref[holder * 4 + column], jnp.int32) > 0
            v = jnp.where(late, v[4:52], v[0:48])
            fold = jnp.concatenate([v[0:24, 256:320], v[24:48, 256:320]], axis=1)
            tile = jnp.concatenate([v[0:48, 0:128], v[0:48, 128:256], fold, jnp.zeros((8, 128), f32)], axis=0)
            part_ref[i, column] = tile.astype(bf16).reshape(NZL, 16, 128)
            if d > 0:
                ycopies[i].append(
                    send(part_ref.at[i, column], ybuf.at[d - 1, i], ys.at[d - 1, i], yr.at[d - 1, i], to_y[d - 1])
                )
    for i in range(4):
        for c in ycopies[i]:
            c.wait()
        v = part_ref[i, y].astype(f32)
        for d in range(3):
            v = v + ybuf[d, i].astype(f32)
        s1[i] = v.astype(bf16)
        lcopies.append([
            send(s1.at[i, lax.rem(z_lo + d, 8)], zbuf.at[d - 1, i], ls.at[d - 1, i], lr.at[d - 1, i], to_l[d - 1])
            for d in (4, 3, 5, 2, 6, 1, 7)
        ])
    for i, step in ((0, 2), (2, 3), (3, 0), (1, 1)):
        for c in lcopies[i]:
            c.wait()
        v = s1[i, z_lo].astype(f32)
        for d in range(7):
            v = v + zbuf[d, i].astype(f32)
        if step == 0:
            own_sum = v
        else:
            if step == 1:
                hcopies[0].wait()
                v = v + hbuf[0].astype(f32)
            s2b[i] = v.astype(bf16)
            hcopies[i] = send(s2b.at[i], hbuf.at[i], hs.at[i], hr.at[i], to_z[3 if step == 3 else 1])
    v = own_sum
    for i in (2, 1):
        hcopies[i].wait()
        v = v + hbuf[i].astype(f32)
    final[...] = (v * (1.0 / SAMPLES)).astype(bf16)

    kept = pltpu.make_async_copy(final, all_ref.at[core, x, z_lo], keep_sem)
    kept.start()
    copies = [
        send(final, all_ref.at[core, x, z_lo], gs.at[d - 1], gr.at[d - 1], to_l[d - 1])
        for d in (4, 3, 5, 2, 6, 1, 7)
    ]
    kept.wait()
    for c in copies:
        c.wait()
    quarter = all_ref.at[core, x]
    copies = {d: send(quarter, quarter, xs.at[d - 1], xr.at[d - 1], to_x[d - 1]) for d in (2, 1, 3)}
    forwards = [send(quarter, quarter, cs.at[0], cr.at[0], other)]
    for d in (1, 3, 2):
        copies[d].wait_recv()
        part = all_ref.at[core, lax.rem(x + 4 - d, 4)]
        forwards.append(send(part, part, cs.at[d], cr.at[d], other))
    for d in (1, 3, 2):
        copies[d].wait_send()
    for c in forwards:
        c.wait()


def run_step(index, tiles, odd, x, cot, bias, first_weight, second_weight):
    dma = pltpu.SemaphoreType.DMA
    v = pltpu.VMEM
    return pl.pallas_call(
        step_kernel,
        out_shape=(
            jax.ShapeDtypeStruct((PIX, C), bf16),
            jax.ShapeDtypeStruct((2, NX, NZL, 16, 128), bf16),
        ),
        in_specs=[SM, SM, SM, VM, VM, VM, VM, VM],
        out_specs=(VM, VM),
        scratch_shapes=[
            v((2, 4, 2, 64, 128), bf16), v((2, NZH * NY, 4, 2, 64, 128), bf16),
            v((9 * C, C), bf16), v((9 * C, C), bf16), v((3, 160, C), bf16),
            v((C, 128), bf16), v((C, 128), bf16), v((C, 128), bf16), v((C, 128), bf16),
            v((8, C, 128), bf16), v((8, C, 128), bf16), v((C, 8 * PIX), bf16),
            v((3, 8, 160, C), bf16), v((9 * C // 8 + 3, 8, C), f32),
            v((NZH, NY, NZL, 16, 128), bf16), v((3, NZH, NZL, 16, 128), bf16),
            v((NZH, NZL, 16, 128), bf16), v((7, NZH, 16, 128), bf16), v((3, 16, 128), bf16),
            v((3, 16, 128), bf16), v((16, 128), bf16),
            dma((2,)), dma((3, 2)), dma((3, 2)), dma((2,)), dma((2,)), dma((3,)), dma((3,)), dma((3, 3)), dma((3, 3)),
            dma((3, 4, 3)), dma((3, 4, 3)), dma((4, 4)), dma((4, 4)), dma((4, 4)), dma((2, 4, 2)),
            dma((3, 4)), dma((3, 4)), dma((7, 4)), dma((7, 4)), dma((3,)), dma((3,)),
            dma((7,)), dma((7,)), dma((3,)), dma((3,)), dma((4,)), dma((4,)), dma,
        ],
        compiler_params=pltpu.CompilerParams(collective_id=0, has_side_effects=True),
        name="step",
    )(index, tiles, odd, x, cot, bias, first_weight, second_weight)


def finish_kernel(out_ref, all_ref, result_ref, first_ref, second_ref):
    result_ref[...] = out_ref[...]
    for kernel, target in ((0, first_ref), (1, second_ref)):
        for q in range(4):
            v = all_ref[kernel, q].astype(f32).reshape(128, 128)
            base, n = QROWS * q, min(QROWS, BLOCK - QROWS * q)
            target[base : base + n, 0:128] = v[0:n]
            target[base : base + n, 128:256] = v[48 : 48 + n]
            target[base : base + 24, 256:320] = v[96:120, 0:64]
            target[base + 24 : base + n, 256:320] = v[96 : 72 + n, 64:128]


def finish(out, everything):
    grad = jax.ShapeDtypeStruct((BLOCK, C), f32)
    return pl.pallas_call(
        finish_kernel,
        out_shape=(jax.ShapeDtypeStruct((PIX, C), bf16), grad, grad),
        in_specs=[VM, VM],
        out_specs=(VM, VM, VM),
        name="finish",
    )(out, everything)


def time_bias(timestep, time_weight):
    half_dim = TEMB // 2
    frequency = jnp.exp(-math.log(10000.0) * jnp.arange(half_dim, dtype=f32) / half_dim)
    angles = timestep.astype(f32) * frequency
    embedded = jnp.concatenate([jnp.cos(angles), jnp.sin(angles)])
    activated = jax.nn.silu(embedded).astype(bf16)
    return jnp.dot(activated[None, :], time_weight, preferred_element_type=f32)


def body(block_input, cotangent, timesteps, owner_map, time_weight, first_weight, second_weight):
    ids = jnp.arange(16, dtype=jnp.int32)
    inverse = jnp.sum((owner_map[None, :] == ids[:, None]).astype(jnp.int32) * ids[None, :], axis=1)
    quarter = lax.rem(lax.axis_index("rep") // 2, 4)
    starts = inverse * BLOCK + quarter.astype(jnp.int32) * QROWS
    bias = time_bias(timesteps[0], time_weight)
    x = block_input.reshape(PIX, C)
    cot = cotangent.reshape(PIX, C)
    out, everything = run_step(owner_map, starts // 8, lax.rem(starts // 4, 2), x, cot, bias, first_weight, second_weight)
    out, first_grad, second_grad = finish(out, everything)
    return out.reshape(1, HEIGHT, WIDTH, C), first_grad, second_grad


def solution(mesh):
    placed = (
        P(("rep", "dom"), None, None, None),
        P(("rep", "dom"), None, None, None),
        P(("rep", "dom")),
        P(),
        P(),
        P("dom", None),
        P("dom", None),
    )
    return jax.shard_map(
        body,
        mesh=mesh,
        in_specs=placed,
        out_specs=(P(("rep", "dom"), None, None, None), P("dom", None), P("dom", None)),
        check_vma=False,
    )
```
